32 devices in a mesh: layer: 4 (over y, x), token: 4 (over z), fhalf: 2 (over core).
Axes of the slice: x: 2, y: 2, z: 4, core: 2. Of those that a mesh axis runs over, the one named last changes fastest.
Arguments:
- hidden_slab: bfloat16 [4096, 32768], P('token', ('layer', 'fhalf')), may hold values from -27 to 27, as said below
- current_block: float32 [32768, 64], P(('layer', 'fhalf')), may hold values from -6 to 6
- direction: float32 [32768, 64], P(('layer', 'fhalf')), may hold values from -3 to 3
Outputs:
- new_block: float32 [32768, 64], P(('layer', 'fhalf'))
- new_direction: float32 [32768, 64], P(('layer', 'fhalf'))
- ritz_values: float32 [64], replicated
The draws below stay inside these ranges and needn't reach their ends.
Inputs may be any that keep to these rules, and one draw needn't show every extreme that they name: `hidden_slab`: hidden states of the joined layers.
All inputs are finite; a program needn't handle non-finite values.
Results may differ from the reference program's by a relative error of at most 0.0023.
The reference program's roundings to bfloat16 on the way (of `block_b`, `block_probe`, `search_b` and `search_probe`) count: a program that leaves them out, or rounds other values in their place, can miss the bound.
Values may be sent and summed in bfloat16 or wider, within the bound.
No kernel may reach another device: no remote copies, remote signals or barrier semaphores. Data moves between devices by JAX's collectives and lax.ppermute only.
A program may use at most 64 MiB of HBM per device.

```python
import math
import jax
import jax.numpy as jnp
from jax import lax

DL = 8192
LAYERS = 4
FEAT = 32768
K = 64
NSUB = 6
TOK_DEV = 1024
TOKENS = 4096


spike_rank = 8


spike_strength = 4.0


def spike_vectors(key):
    columns = LAYERS * DL
    return jnp.clip(jax.random.normal(jax.random.fold_in(key, 101), (spike_rank, columns), jnp.float32), -3.0, 3.0)


def draw_hidden_slab(key, part):
    columns = LAYERS * DL
    first_key, second_key = jax.random.split(jax.random.fold_in(key, 11), 2)
    amp_key, segment_key = jax.random.split(jax.random.fold_in(key, 23), 2)
    column_scale = jnp.exp(jax.random.uniform(second_key, (columns,), jnp.float32, math.log(0.15), math.log(1.5)))
    layer_index = (jnp.arange(columns) // DL).astype(jnp.float32)
    depth_scale = 1.0 + 2.0 * layer_index / max(LAYERS - 1, 1)
    segment_count = TOKENS // TOK_DEV
    segment_scale = jnp.exp(jax.random.uniform(segment_key, (segment_count, spike_rank), jnp.float32, math.log(0.25), math.log(4.0)))
    segment_rows = jnp.repeat(segment_scale, TOK_DEV, axis=0)
    base = jnp.clip(jax.random.normal(first_key, (TOKENS, columns), jnp.float32), -6.0, 6.0)
    amplitude = jnp.clip(jax.random.normal(amp_key, (TOKENS, spike_rank), jnp.float32), -4.0, 4.0)
    vectors = spike_vectors(key)
    weights = amplitude * segment_rows * (spike_strength / math.sqrt(columns))
    spike_part = jnp.zeros((TOKENS, columns), jnp.float32)
    for index_r in range(spike_rank):
        spike_part = spike_part + weights[:, index_r:index_r + 1] * vectors[index_r][None, :]
    values = base * (column_scale * depth_scale)[None, :] + spike_part
    return jnp.clip(values, -27.0, 27.0).astype(jnp.bfloat16)


def draw_direction(key, part):
    columns = LAYERS * DL
    noise_key = jax.random.fold_in(key, 31)
    mix_key = jax.random.fold_in(key, 37)
    noise = jnp.clip(jax.random.normal(noise_key, (columns, K), jnp.float32), -6.0, 6.0)
    mixing = 0.17 * jnp.clip(jax.random.normal(mix_key, (spike_rank, K), jnp.float32), -4.0, 4.0)
    vectors = spike_vectors(key)
    values = 0.5 * noise
    for index_r in range(spike_rank):
        values = values + vectors[index_r][:, None] * mixing[index_r][None, :]
    return jnp.clip(values, -3.0, 3.0)


def steps_of(rng, shape, cuts, low, high):
    level, own = 1.0, jax.random.fold_in(rng, 6)
    for axis_at, blocks in cuts:
        steps = jnp.exp(jax.random.uniform(jax.random.fold_in(own, axis_at), (blocks,), jnp.float32, low / len(cuts), high / len(cuts)))
        level = level * jnp.repeat(steps, shape[axis_at] // blocks).reshape([-1 if axis == axis_at else 1 for axis in range(len(shape))])
    return level


def centred(stream_key, extent, deviation, most, pieces=(), held_as=jnp.bfloat16):
    values = deviation * jax.random.normal(stream_key, extent, jnp.float32)
    if pieces:
        values = values * steps_of(stream_key, extent, pieces, -0.22, 0.18)
    return jnp.clip(values, -most, most).astype(held_as)


def setup_inputs(seed: int = 0) -> dict:
    streams_of = jax.random.split(jax.random.key(seed), 4)
    hidden_slab = draw_hidden_slab(jax.random.fold_in(streams_of[3], 71), 0)
    current_block = centred(streams_of[1], (FEAT, K), 1.0, 6.0, ((0, 8),), jnp.float32)
    direction = draw_direction(jax.random.fold_in(streams_of[3], 71), 0)
    return {"hidden_slab": hidden_slab, "current_block": current_block, "direction": direction}


def exact_product(left, right):
    return jnp.dot(left.astype(jnp.float32), right.astype(jnp.float32), precision=lax.Precision.HIGHEST, preferred_element_type=jnp.float32)

def exact_transposed(left, right):
    return lax.dot_general(left.astype(jnp.float32), right.astype(jnp.float32), (((0,), (0,)), ((), ())), precision=lax.Precision.HIGHEST, preferred_element_type=jnp.float32)

def contract_tokens(slab_part, probe_rows):
    return lax.dot_general(slab_part.astype(jnp.float32), probe_rows.astype(jnp.float32), (((0,), (0,)), ((), ())), preferred_element_type=jnp.float32)

def whiten_of(gram_matrix):
    lower_factor = jnp.linalg.cholesky(gram_matrix)
    identity = jnp.eye(gram_matrix.shape[0], dtype=gram_matrix.dtype)
    inverse = lax.linalg.triangular_solve(lower_factor, identity, left_side=True, lower=True)
    return inverse.T

def subspace_ritz(matrix, columns, sweeps):
    coeffs = jnp.eye(matrix.shape[0], columns, dtype=matrix.dtype)
    for turn_index in range(sweeps):
        coeffs = exact_product(matrix, coeffs)
        coeffs = exact_product(coeffs, whiten_of(exact_transposed(coeffs, coeffs)))
    return coeffs

def reference(hidden_slab, current_block, direction):
    block_b = current_block.astype(jnp.bfloat16)
    block_probe = jnp.dot(hidden_slab.astype(jnp.float32), block_b.astype(jnp.float32), preferred_element_type=jnp.float32).astype(jnp.bfloat16)
    block_image = contract_tokens(hidden_slab, block_probe) / TOKENS
    ritz_block = exact_transposed(current_block, block_image) / FEAT
    residual = block_image - exact_product(current_block, ritz_block)
    search_basis = jnp.concatenate([current_block, residual, direction], axis=1)
    gram_matrix = exact_transposed(search_basis, search_basis) / FEAT
    whiten = whiten_of(gram_matrix)
    search_b = jnp.concatenate([residual, direction], axis=1).astype(jnp.bfloat16)
    search_probe = jnp.dot(hidden_slab.astype(jnp.float32), search_b.astype(jnp.float32), preferred_element_type=jnp.float32).astype(jnp.bfloat16)
    search_image = contract_tokens(hidden_slab, search_probe) / TOKENS
    ritz_raw = exact_transposed(search_basis, jnp.concatenate([block_image, search_image], axis=1)) / FEAT
    ritz_matrix = exact_transposed(whiten, exact_product(ritz_raw, whiten))
    ritz_matrix = 0.5 * (ritz_matrix + ritz_matrix.T)
    coeffs = subspace_ritz(ritz_matrix, K, NSUB)
    ritz_values = jnp.sum(coeffs * exact_product(ritz_matrix, coeffs), axis=0)
    new_block = exact_product(search_basis, exact_product(whiten, coeffs))
    new_direction = exact_product(search_basis, exact_product(whiten[:, K:], coeffs[K:, :]))
    return (new_block, new_direction, ritz_values)
```

```python
import jax
import jax.numpy as jnp
from jax import lax
from jax.sharding import PartitionSpec as P

NSUB = 6
HIGHEST = lax.Precision.HIGHEST


def exact_product(left, right):
    return jnp.dot(left, right, precision=HIGHEST, preferred_element_type=jnp.float32)


def exact_transposed(left, right):
    return lax.dot_general(
        left, right, (((0,), (0,)), ((), ())), precision=HIGHEST, preferred_element_type=jnp.float32
    )


def exact_rows(left, right):
    return lax.dot_general(
        left, right, (((1,), (1,)), ((), ())), precision=HIGHEST, preferred_element_type=jnp.float32
    )


def whiten_of(gram_matrix):
    lower_factor = jnp.linalg.cholesky(gram_matrix)
    identity = jnp.eye(gram_matrix.shape[0], dtype=gram_matrix.dtype)
    inverse = lax.linalg.triangular_solve(lower_factor, identity, left_side=True, lower=True)
    return inverse.T


def subspace_ritz(matrix, columns, sweeps):
    coeffs = jnp.eye(matrix.shape[0], columns, dtype=matrix.dtype)
    for turn_index in range(sweeps):
        coeffs = exact_product(matrix, coeffs)
        coeffs = exact_product(coeffs, whiten_of(exact_transposed(coeffs, coeffs)))
    return coeffs


def swap(value, axis, step):
    return lax.ppermute(value, axis, [(i, i ^ step) for i in range(lax.axis_size(axis))])


def steps_of(axis):
    size = lax.axis_size(axis)
    if size & (size - 1):
        raise ValueError(axis)
    return [1 << bit for bit in range(size.bit_length() - 1)]


def reduce_all(value, axis):
    for step in steps_of(axis):
        value = value + swap(value, axis, step)
    return value


def side_of(axis, step):
    return (lax.axis_index(axis) // step) % 2


def reduce_halves(value, axis):
    for step in steps_of(axis):
        half = value.shape[1] // 2
        side = side_of(axis, step)
        kept = lax.dynamic_slice_in_dim(value, side * half, half, 1)
        sent = lax.dynamic_slice_in_dim(value, (1 - side) * half, half, 1)
        value = kept + swap(sent, axis, step)
    return value


def own_part(value, axis):
    for step in steps_of(axis):
        half = value.shape[1] // 2
        value = lax.dynamic_slice_in_dim(value, side_of(axis, step) * half, half, 1)
    return value


def gather_halves(value, axis):
    for step in reversed(steps_of(axis)):
        other = swap(value, axis, step)
        first = side_of(axis, step) == 0
        value = jnp.concatenate([jnp.where(first, value, other), jnp.where(first, other, value)], axis=1)
    return value


def local(hidden_slab, current_block, direction):
    tok_rows, half_width = hidden_slab.shape
    cols = current_block.shape[1]
    feat_total = half_width * lax.axis_size("layer") * lax.axis_size("fhalf")
    token_total = tok_rows * lax.axis_size("token")
    x_rows = current_block.T
    d_rows = direction.T
    start_b = jnp.concatenate([x_rows, d_rows], axis=0).astype(jnp.bfloat16)
    start_part = lax.dot_general(
        start_b, hidden_slab, (((1,), (1,)), ((), ())), preferred_element_type=jnp.float32
    )
    x_probe = reduce_all(reduce_halves(start_part[:cols], "fhalf"), "layer")
    x_probe_b = x_probe.astype(jnp.bfloat16)
    block_probe = gather_halves(x_probe_b, "fhalf")
    ritz_block = lax.dot_general(
        block_probe, block_probe, (((1,), (1,)), ((), ())), preferred_element_type=jnp.float32
    )
    ritz_block = reduce_all(ritz_block, "token") / (token_total * feat_total)
    image_part = jnp.dot(block_probe, hidden_slab, preferred_element_type=jnp.float32)
    image = reduce_halves(image_part, "token") / token_total
    x_own = own_part(x_rows, "token")
    d_own = own_part(d_rows, "token")
    residual = image - exact_transposed(ritz_block, x_own)
    residual_b = residual.astype(jnp.bfloat16)
    residual_lo = (residual - residual_b.astype(jnp.float32)).astype(jnp.bfloat16)
    search_b = gather_halves(residual_b, "token")
    search_lo = gather_halves(residual_lo, "token")
    d_probe = reduce_all(reduce_halves(start_part[cols:], "fhalf"), "layer")
    own = jnp.concatenate([x_own, residual, d_own], axis=0)
    gram_part = exact_rows(own, own)
    gram_matrix = reduce_all(reduce_all(gram_part, "layer"), "fhalf")
    gram_matrix = reduce_all(gram_matrix, "token") / feat_total
    whiten = whiten_of(gram_matrix)
    r_part = lax.dot_general(
        search_b, hidden_slab, (((1,), (1,)), ((), ())), preferred_element_type=jnp.float32
    )
    r_probe = reduce_all(reduce_halves(r_part, "fhalf"), "layer")
    probes = jnp.concatenate([x_probe, r_probe, d_probe], axis=0)
    probes_b = probes.astype(jnp.bfloat16).astype(jnp.float32)
    ritz_part = exact_rows(probes, probes_b)
    ritz_raw = reduce_all(reduce_all(ritz_part, "fhalf"), "token") / (token_total * feat_total)
    ritz_matrix = exact_transposed(whiten, exact_product(ritz_raw, whiten))
    ritz_matrix = 0.5 * (ritz_matrix + ritz_matrix.T)
    coeffs = subspace_ritz(ritz_matrix, cols, NSUB)
    ritz_values = jnp.sum(coeffs * exact_product(ritz_matrix, coeffs), axis=0)
    all_coeffs = jnp.concatenate(
        [exact_product(whiten, coeffs), exact_product(whiten[:, cols:], coeffs[cols:, :])], axis=1
    )
    residual_rows = search_b.astype(jnp.float32) + search_lo.astype(jnp.float32)
    search_basis = jnp.concatenate([x_rows, residual_rows, d_rows], axis=0)
    moved = exact_transposed(all_coeffs, search_basis)
    return (moved[:cols].T, moved[cols:].T, ritz_values)


def solution(mesh):
    return jax.shard_map(
        local,
        mesh=mesh,
        in_specs=(
            P("token", ("layer", "fhalf")),
            P(("layer", "fhalf"), None),
            P(("layer", "fhalf"), None),
        ),
        out_specs=(P(("layer", "fhalf"), None), P(("layer", "fhalf"), None), P()),
        check_vma=False,
    )
```

```python
import jax
import jax.numpy as jnp
from jax import lax
from jax.experimental import pallas as pl
from jax.experimental.pallas import tpu as pltpu
from jax.sharding import PartitionSpec as P

NSUB = 6
SPREAD = 1e-4
LARGE = 1e30
HIGHEST = lax.Precision.HIGHEST


def exact_transposed(left, right):
    return lax.dot_general(
        left, right, (((0,), (0,)), ((), ())), precision=HIGHEST, preferred_element_type=jnp.float32
    )


def exact_rows(left, right):
    return lax.dot_general(
        left, right, (((1,), (1,)), ((), ())), precision=HIGHEST, preferred_element_type=jnp.float32
    )


def product(left, right):
    return jnp.dot(left, right, precision=HIGHEST, preferred_element_type=jnp.float32)


def identity(rows, columns):
    down = lax.broadcasted_iota(jnp.int32, (rows, columns), 0)
    across = lax.broadcasted_iota(jnp.int32, (rows, columns), 1)
    return jnp.where(down == across, 1.0, 0.0).astype(jnp.float32)


def factor_inverse(gram):
    size = gram.shape[0]
    wide = jnp.concatenate([gram, identity(size, size)], axis=1)
    tile = (8, 2 * size)
    rows = [wide[8 * g : 8 * g + 8] for g in range(size // 8)]
    sub = lax.broadcasted_iota(jnp.int32, tile, 0)
    done = []
    low = high = total = None
    for g in range(size // 8):
        live = rows[g:]
        panel = [[jnp.broadcast_to(r[:, 8 * g + j : 8 * g + j + 1], tile) for r in live] for j in range(8)]
        scale = None
        for j in range(8):
            head = panel[j][0]
            pivot = jnp.broadcast_to(head[j : j + 1], tile)
            inverse = 1.0 / pivot
            row = jnp.broadcast_to(live[0][j : j + 1], tile)
            factors = [value * inverse for value in panel[j]]
            factors[0] = jnp.where(sub > j, factors[0], 0.0)
            for i in range(j + 1, 8):
                other = jnp.broadcast_to(head[i : i + 1], tile)
                panel[i] = [value - f * other for value, f in zip(panel[i], factors)]
            live = [value - f * row for value, f in zip(live, factors)]
            scale = pivot if scale is None else jnp.where(sub >= j, pivot, scale)
            low = pivot if low is None else jnp.minimum(low, pivot)
            high = pivot if high is None else jnp.maximum(high, pivot)
            total = pivot if total is None else total + pivot
        rows[g:] = live
        done.append(live[0] * lax.rsqrt(scale))
    return jnp.concatenate(done, axis=0)[:, size:], low, high, total


def whiten_kernel(gram_ref, out_ref):
    cols = gram_ref.shape[0] // 3

    def block(i, j):
        return gram_ref[cols * i : cols * i + cols, cols * j : cols * j + cols]

    first = factor_inverse(block(0, 0))[0]
    lower_10 = exact_rows(block(1, 0), first)
    lower_20 = exact_rows(block(2, 0), first)
    second = factor_inverse(block(1, 1) - exact_rows(lower_10, lower_10))[0]
    lower_21 = exact_rows(block(2, 1) - exact_rows(lower_20, lower_10), second)
    third = factor_inverse(block(2, 2) - exact_rows(lower_20, lower_20) - exact_rows(lower_21, lower_21))[0]
    inverse_10 = -product(second, product(lower_10, first))
    inverse_20 = -product(third, product(lower_20, first) + product(lower_21, inverse_10))
    inverse_21 = -product(third, product(lower_21, second))
    zero = jnp.zeros((cols, cols), jnp.float32)
    out_ref[...] = jnp.concatenate(
        [
            jnp.concatenate([first, zero, zero], axis=1),
            jnp.concatenate([inverse_10, second, zero], axis=1),
            jnp.concatenate([inverse_20, inverse_21, third], axis=1),
        ],
        axis=0,
    )


def whiten_rows(gram_matrix):
    return pl.pallas_call(
        whiten_kernel, out_shape=jax.ShapeDtypeStruct(gram_matrix.shape, jnp.float32), name="whiten"
    )(gram_matrix)


def ritz_kernel(whiten_ref, raw_ref, coeffs_ref, values_ref, matrix_ref, power_ref, turned_ref, basis_ref):
    size, cols = turned_ref.shape
    power_ref[...] = product(whiten_ref[...], raw_ref[...])
    matrix_ref[...] = exact_rows(power_ref[...], whiten_ref[...])
    matrix_ref[...] = 0.5 * (matrix_ref[...] + matrix_ref[...].T)
    power_ref[...] = product(matrix_ref[...], matrix_ref[...])
    power_ref[...] = product(power_ref[...], matrix_ref[...])

    def sweep(step_ref, count):
        basis_ref[...] = identity(size, cols)

        def turn(_, good):
            turned_ref[...] = product(step_ref[...], basis_ref[...])
            turned = turned_ref[...]
            inverse, low, high, total = factor_inverse(exact_transposed(turned, turned))
            basis_ref[...] = exact_rows(turned_ref[...], inverse)
            fine = jnp.logical_and(low > SPREAD * high, total < LARGE)
            return jnp.minimum(good, jnp.where(fine, 1.0, 0.0))

        return lax.fori_loop(0, count, turn, jnp.ones((8, 2 * cols), jnp.float32))

    good = jnp.min(sweep(power_ref, NSUB // 3))

    @pl.when(good < 0.5)
    def _():
        sweep(matrix_ref, NSUB)

    values_ref[...] = jnp.sum(
        basis_ref[...] * product(matrix_ref[...], basis_ref[...]), axis=0, keepdims=True
    )
    down = lax.broadcasted_iota(jnp.int32, (size, cols), 0)
    coeffs_ref[:, :cols] = exact_transposed(whiten_ref[...], basis_ref[...])
    coeffs_ref[:, cols:] = exact_transposed(
        whiten_ref[...], jnp.where(down >= cols, basis_ref[...], 0.0)
    )


def ritz_of(whiten, ritz_raw):
    size = ritz_raw.shape[0]
    cols = size // 3
    return pl.pallas_call(
        ritz_kernel,
        out_shape=(
            jax.ShapeDtypeStruct((size, 2 * cols), jnp.float32),
            jax.ShapeDtypeStruct((1, cols), jnp.float32),
        ),
        scratch_shapes=[
            pltpu.VMEM((size, size), jnp.float32),
            pltpu.VMEM((size, size), jnp.float32),
            pltpu.VMEM((size, cols), jnp.float32),
            pltpu.VMEM((size, cols), jnp.float32),
        ],
        name="ritz",
    )(whiten, ritz_raw)


def rounded(value):
    return lax.reduce_precision(value, exponent_bits=8, mantissa_bits=7)


def swap(value, axis, step):
    return lax.ppermute(value, axis, [(i, i ^ step) for i in range(lax.axis_size(axis))])


def steps_of(axis):
    size = lax.axis_size(axis)
    if size & (size - 1):
        raise ValueError(axis)
    return [1 << bit for bit in range(size.bit_length() - 1)]


def reduce_all(value, axis):
    for step in steps_of(axis):
        value = value + swap(value, axis, step)
    return value


def side_of(axis, step):
    return (lax.axis_index(axis) // step) % 2


def reduce_halves(value, axis):
    for step in steps_of(axis):
        half = value.shape[1] // 2
        side = side_of(axis, step)
        kept = lax.dynamic_slice_in_dim(value, side * half, half, 1)
        sent = lax.dynamic_slice_in_dim(value, (1 - side) * half, half, 1)
        value = kept + swap(sent, axis, step)
    return value


def own_part(value, axis):
    for step in steps_of(axis):
        half = value.shape[1] // 2
        value = lax.dynamic_slice_in_dim(value, side_of(axis, step) * half, half, 1)
    return value


def gather_halves(value, axis):
    for step in reversed(steps_of(axis)):
        other = swap(value, axis, step)
        first = side_of(axis, step) == 0
        value = jnp.concatenate([jnp.where(first, value, other), jnp.where(first, other, value)], axis=1)
    return value


def local(hidden_slab, current_block, direction):
    tok_rows, half_width = hidden_slab.shape
    cols = current_block.shape[1]
    feat_total = half_width * lax.axis_size("layer") * lax.axis_size("fhalf")
    token_total = tok_rows * lax.axis_size("token")
    x_rows = current_block.T
    d_rows = direction.T
    start_b = jnp.concatenate([x_rows, d_rows], axis=0).astype(jnp.bfloat16)
    start_part = lax.dot_general(
        start_b, hidden_slab, (((1,), (1,)), ((), ())), preferred_element_type=jnp.float32
    )
    x_probe = reduce_all(reduce_halves(start_part[:cols], "fhalf"), "layer")
    x_probe_b = x_probe.astype(jnp.bfloat16)
    block_probe = gather_halves(x_probe_b, "fhalf")
    ritz_block = lax.dot_general(
        block_probe, block_probe, (((1,), (1,)), ((), ())), preferred_element_type=jnp.float32
    )
    ritz_block = reduce_all(ritz_block, "token") / (token_total * feat_total)
    image_part = jnp.dot(block_probe, hidden_slab, preferred_element_type=jnp.float32)
    image = reduce_halves(image_part, "token") / token_total
    x_own = own_part(x_rows, "token")
    d_own = own_part(d_rows, "token")
    residual = image - exact_transposed(ritz_block, x_own)
    residual_hi = rounded(residual)
    residual_b = residual_hi.astype(jnp.bfloat16)
    residual_lo = (residual - residual_hi).astype(jnp.bfloat16)
    search_b = gather_halves(residual_b, "token")
    search_lo = gather_halves(residual_lo, "token")
    d_probe = reduce_all(reduce_halves(start_part[cols:], "fhalf"), "layer")
    own = jnp.concatenate([x_own, residual, d_own], axis=0)
    gram_part = exact_rows(own, own)
    gram_matrix = reduce_all(reduce_all(gram_part, "layer"), "fhalf")
    gram_matrix = reduce_all(gram_matrix, "token") / feat_total
    whiten = whiten_rows(gram_matrix)
    r_part = lax.dot_general(
        search_b, hidden_slab, (((1,), (1,)), ((), ())), preferred_element_type=jnp.float32
    )
    r_probe = reduce_all(reduce_halves(r_part, "fhalf"), "layer")
    probes = jnp.concatenate([x_probe, r_probe, d_probe], axis=0)
    ritz_part = exact_rows(probes, rounded(probes))
    ritz_raw = reduce_all(reduce_all(ritz_part, "fhalf"), "token") / (token_total * feat_total)
    all_coeffs, ritz_values = ritz_of(whiten, ritz_raw)
    residual_rows = search_b.astype(jnp.float32) + search_lo.astype(jnp.float32)
    search_basis = jnp.concatenate([x_rows, residual_rows, d_rows], axis=0)
    moved = exact_transposed(all_coeffs, search_basis)
    return (moved[:cols].T, moved[cols:].T, ritz_values[0])


def solution(mesh):
    return jax.shard_map(
        local,
        mesh=mesh,
        in_specs=(
            P("token", ("layer", "fhalf")),
            P(("layer", "fhalf"), None),
            P(("layer", "fhalf"), None),
        ),
        out_specs=(P(("layer", "fhalf"), None), P(("layer", "fhalf"), None), P()),
        check_vma=False,
    )
```

```python
import jax
import jax.numpy as jnp
from jax import lax
from jax.experimental import pallas as pl
from jax.experimental.pallas import tpu as pltpu
from jax.sharding import PartitionSpec as P

NSUB = 6
CHUNKS = 2
SPREAD = 1e-4
LARGE = 1e30
HIGHEST = lax.Precision.HIGHEST


def exact_transposed(left, right):
    return lax.dot_general(
        left, right, (((0,), (0,)), ((), ())), precision=HIGHEST, preferred_element_type=jnp.float32
    )


def exact_rows(left, right):
    return lax.dot_general(
        left, right, (((1,), (1,)), ((), ())), precision=HIGHEST, preferred_element_type=jnp.float32
    )


def product(left, right):
    return jnp.dot(left, right, precision=HIGHEST, preferred_element_type=jnp.float32)


def identity(rows, columns):
    down = lax.broadcasted_iota(jnp.int32, (rows, columns), 0)
    across = lax.broadcasted_iota(jnp.int32, (rows, columns), 1)
    return jnp.where(down == across, 1.0, 0.0).astype(jnp.float32)


def factor_inverse(gram):
    size = gram.shape[0]
    wide = jnp.concatenate([gram, identity(size, size)], axis=1)
    tile = (8, 2 * size)
    rows = [wide[8 * g : 8 * g + 8] for g in range(size // 8)]
    sub = lax.broadcasted_iota(jnp.int32, tile, 0)
    done = []
    low = high = total = None
    for g in range(size // 8):
        live = rows[g:]
        panel = [[jnp.broadcast_to(r[:, 8 * g + j : 8 * g + j + 1], tile) for r in live] for j in range(8)]
        scale = None
        for j in range(8):
            head = panel[j][0]
            pivot = jnp.broadcast_to(head[j : j + 1], tile)
            inverse = 1.0 / pivot
            row = jnp.broadcast_to(live[0][j : j + 1], tile)
            factors = [value * inverse for value in panel[j]]
            factors[0] = jnp.where(sub > j, factors[0], 0.0)
            for i in range(j + 1, 8):
                other = jnp.broadcast_to(head[i : i + 1], tile)
                panel[i] = [value - f * other for value, f in zip(panel[i], factors)]
            live = [value - f * row for value, f in zip(live, factors)]
            scale = pivot if scale is None else jnp.where(sub >= j, pivot, scale)
            low = pivot if low is None else jnp.minimum(low, pivot)
            high = pivot if high is None else jnp.maximum(high, pivot)
            total = pivot if total is None else total + pivot
        rows[g:] = live
        done.append(live[0] * lax.rsqrt(scale))
    return jnp.concatenate(done, axis=0)[:, size:], low, high, total


def whiten_given_kernel(gram_ref, out_ref):
    cols = gram_ref.shape[0] // 2
    first = factor_inverse(gram_ref[:cols, :cols])[0]
    lower = exact_rows(gram_ref[cols:, :cols], first)
    second = factor_inverse(gram_ref[cols:, cols:] - exact_rows(lower, lower))[0]
    out_ref[:cols, :cols] = first
    out_ref[:cols, cols:] = jnp.zeros((cols, cols), jnp.float32)
    out_ref[cols:, :cols] = -product(second, product(lower, first))
    out_ref[cols:, cols:] = second


def whiten_given(gram_matrix):
    return pl.pallas_call(
        whiten_given_kernel,
        out_shape=jax.ShapeDtypeStruct(gram_matrix.shape, jnp.float32),
        cost_estimate=pl.CostEstimate(flops=4_000_000_000, transcendentals=0, bytes_accessed=131072),
        name="whiten_given",
    )(gram_matrix)


def whiten_rest_kernel(given_ref, gram_ref, out_ref):
    cols, size = gram_ref.shape
    lower = exact_rows(gram_ref[:, : size - cols], given_ref[...])
    last = factor_inverse(gram_ref[:, size - cols :] - exact_rows(lower, lower))[0]
    out_ref[:, : size - cols] = -product(last, product(lower, given_ref[...]))
    out_ref[:, size - cols :] = last


def whiten_rest(given, gram_rows):
    return pl.pallas_call(
        whiten_rest_kernel,
        out_shape=jax.ShapeDtypeStruct(gram_rows.shape, jnp.float32),
        cost_estimate=pl.CostEstimate(flops=3_000_000_000, transcendentals=0, bytes_accessed=131072),
        name="whiten_rest",
    )(given, gram_rows)


def ritz_kernel(
    given_ref, rest_ref, raw_given_ref, raw_rest_ref, coeffs_ref, values_ref,
    whiten_ref, matrix_ref, power_ref, turned_ref, basis_ref,
):
    size, cols = turned_ref.shape
    rest = size - cols
    whiten_ref[:rest, :rest] = given_ref[...]
    whiten_ref[:rest, rest:] = jnp.zeros((rest, cols), jnp.float32)
    whiten_ref[rest:, :] = rest_ref[...]
    matrix_ref[:rest, :rest] = 0.5 * (raw_given_ref[...] + raw_given_ref[...].T)
    matrix_ref[rest:, :] = raw_rest_ref[...]
    matrix_ref[:rest, rest:] = raw_rest_ref[:, :rest].T
    power_ref[...] = product(whiten_ref[...], matrix_ref[...])
    matrix_ref[...] = exact_rows(power_ref[...], whiten_ref[...])
    matrix_ref[...] = 0.5 * (matrix_ref[...] + matrix_ref[...].T)
    power_ref[...] = product(matrix_ref[...], matrix_ref[...])
    power_ref[...] = product(power_ref[...], matrix_ref[...])

    def sweep(step_ref, count):
        basis_ref[...] = identity(size, cols)

        def turn(_, good):
            turned_ref[...] = product(step_ref[...], basis_ref[...])
            turned = turned_ref[...]
            inverse, low, high, total = factor_inverse(exact_transposed(turned, turned))
            basis_ref[...] = exact_rows(turned_ref[...], inverse)
            fine = jnp.logical_and(low > SPREAD * high, total < LARGE)
            return jnp.minimum(good, jnp.where(fine, 1.0, 0.0))

        return lax.fori_loop(0, count, turn, jnp.ones((8, 2 * cols), jnp.float32))

    good = jnp.min(sweep(power_ref, NSUB // 3))

    @pl.when(good < 0.5)
    def _():
        sweep(matrix_ref, NSUB)

    values_ref[...] = jnp.sum(
        basis_ref[...] * product(matrix_ref[...], basis_ref[...]), axis=0, keepdims=True
    )
    down = lax.broadcasted_iota(jnp.int32, (size, cols), 0)
    coeffs_ref[:, :cols] = exact_transposed(whiten_ref[...], basis_ref[...])
    coeffs_ref[:, cols:] = exact_transposed(
        whiten_ref[...], jnp.where(down >= cols, basis_ref[...], 0.0)
    )


def ritz_of(given, rest, raw_given, raw_rest):
    cols, size = rest.shape
    return pl.pallas_call(
        ritz_kernel,
        out_shape=(
            jax.ShapeDtypeStruct((size, 2 * cols), jnp.float32),
            jax.ShapeDtypeStruct((1, cols), jnp.float32),
        ),
        scratch_shapes=[
            pltpu.VMEM((size, size), jnp.float32),
            pltpu.VMEM((size, size), jnp.float32),
            pltpu.VMEM((size, size), jnp.float32),
            pltpu.VMEM((size, cols), jnp.float32),
            pltpu.VMEM((size, cols), jnp.float32),
        ],
        cost_estimate=pl.CostEstimate(flops=10_000_000_000, transcendentals=0, bytes_accessed=524288),
        name="ritz",
    )(given, rest, raw_given, raw_rest)


def rounded(value):
    return lax.reduce_precision(value, exponent_bits=8, mantissa_bits=7)


def swap(value, axis, step):
    return lax.ppermute(value, axis, [(i, i ^ step) for i in range(lax.axis_size(axis))])


def steps_of(axis):
    size = lax.axis_size(axis)
    if size & (size - 1):
        raise ValueError(axis)
    return [1 << bit for bit in range(size.bit_length() - 1)]


def reduce_all(value, axis):
    size = lax.axis_size(axis)
    if size == 4:
        near, far, across = (swap(value, axis, step) for step in (1, 2, 3))
        return (value + near) + (far + across)
    for step in steps_of(axis):
        value = value + swap(value, axis, step)
    return value


def side_of(axis, step):
    return (lax.axis_index(axis) // step) % 2


def reduce_halves(value, axis):
    for step in steps_of(axis):
        half = value.shape[1] // 2
        side = side_of(axis, step)
        kept = lax.dynamic_slice_in_dim(value, side * half, half, 1)
        sent = lax.dynamic_slice_in_dim(value, (1 - side) * half, half, 1)
        value = kept + swap(sent, axis, step)
    return value


def own_part(value, axis):
    for step in steps_of(axis):
        half = value.shape[1] // 2
        value = lax.dynamic_slice_in_dim(value, side_of(axis, step) * half, half, 1)
    return value


def gather_halves(value, axis):
    for step in reversed(steps_of(axis)):
        other = swap(value, axis, step)
        first = side_of(axis, step) == 0
        value = jnp.concatenate([jnp.where(first, value, other), jnp.where(first, other, value)], axis=1)
    return value


def probe_of(rows_b, slab_part):
    return lax.dot_general(
        rows_b, slab_part, (((1,), (1,)), ((), ())), preferred_element_type=jnp.float32
    )


def local(hidden_slab, current_block, direction):
    tok_rows, half_width = hidden_slab.shape
    cols = current_block.shape[1]
    feat_total = half_width * lax.axis_size("layer") * lax.axis_size("fhalf")
    token_total = tok_rows * lax.axis_size("token")
    x_rows = current_block.T
    d_rows = direction.T
    given_rows = jnp.concatenate([x_rows, d_rows], axis=0)
    chunk = half_width // CHUNKS
    slabs = [hidden_slab[:, chunk * c : chunk * c + chunk] for c in range(CHUNKS)]
    given_part = probe_of(given_rows.astype(jnp.bfloat16), hidden_slab)
    x_probe = reduce_all(reduce_halves(given_part[:cols], "fhalf"), "layer")
    x_probe_b = rounded(x_probe)
    block_probe = gather_halves(x_probe_b.astype(jnp.bfloat16), "fhalf")
    ritz_block = reduce_all(probe_of(block_probe, block_probe), "token") / (token_total * feat_total)
    images = [
        reduce_halves(jnp.dot(block_probe, slab, preferred_element_type=jnp.float32), "token")
        for slab in slabs
    ]
    given_own = [
        own_part(given_rows[:, chunk * c : chunk * c + chunk], "token") for c in range(CHUNKS)
    ]
    residuals = [
        image / token_total - exact_transposed(ritz_block, own[:cols])
        for image, own in zip(images, given_own)
    ]
    highs = [rounded(residual) for residual in residuals]
    search = [gather_halves(high.astype(jnp.bfloat16), "token") for high in highs]
    r_part = sum(probe_of(rows, slab) for rows, slab in zip(search, slabs))
    r_probe = reduce_all(reduce_halves(r_part, "fhalf"), "layer")
    d_half = reduce_halves(given_part[cols:], "fhalf")
    d_probe = reduce_all(d_half, "layer")
    gram_given = reduce_all(reduce_all(exact_rows(given_rows, given_rows), "fhalf"), "layer")
    given_inverse = whiten_given(gram_given / feat_total)
    given_probe = jnp.concatenate([x_probe, d_probe], axis=0)
    given_probe_b = jnp.concatenate([x_probe_b, rounded(d_probe)], axis=0)
    raw_given = exact_rows(given_probe, given_probe_b)
    raw_given = reduce_all(reduce_all(raw_given, "fhalf"), "token") / (token_total * feat_total)
    gram_rest = sum(
        exact_rows(residual, jnp.concatenate([own, residual], axis=0))
        for residual, own in zip(residuals, given_own)
    )
    gram_rest = reduce_all(reduce_all(reduce_all(gram_rest, "fhalf"), "layer"), "token")
    rest_inverse = whiten_rest(given_inverse, gram_rest / feat_total)
    r_probe_b = rounded(r_probe)
    raw_rest = jnp.concatenate(
        [
            0.5 * (exact_rows(r_probe, given_probe_b) + exact_rows(r_probe_b, given_probe)),
            exact_rows(r_probe, r_probe_b),
        ],
        axis=1,
    )
    raw_rest = reduce_all(reduce_all(raw_rest, "fhalf"), "token") / (token_total * feat_total)
    all_coeffs, ritz_values = ritz_of(given_inverse, rest_inverse, raw_given, raw_rest)
    lows = [
        gather_halves((residual - high).astype(jnp.bfloat16), "token")
        for residual, high in zip(residuals, highs)
    ]
    residual_rows = jnp.concatenate(
        [high.astype(jnp.float32) + low.astype(jnp.float32) for high, low in zip(search, lows)], axis=1
    )
    search_basis = jnp.concatenate([given_rows, residual_rows], axis=0)
    new_block = exact_transposed(all_coeffs[:, :cols], search_basis)
    new_direction = exact_transposed(all_coeffs[:, cols:], search_basis)
    return (new_block.T, new_direction.T, ritz_values[0])


def solution(mesh):
    return jax.shard_map(
        local,
        mesh=mesh,
        in_specs=(
            P("token", ("layer", "fhalf")),
            P(("layer", "fhalf"), None),
            P(("layer", "fhalf"), None),
        ),
        out_specs=(P(("layer", "fhalf"), None), P(("layer", "fhalf"), None), P()),
        check_vma=False,
    )
```

```python
import jax
import jax.numpy as jnp
from jax import lax
from jax.experimental import pallas as pl
from jax.experimental.pallas import tpu as pltpu
from jax.sharding import PartitionSpec as P

NSUB = 6
CHUNKS = 2
SPREAD = 1e-4
LARGE = 1e30
HIGHEST = lax.Precision.HIGHEST


def exact_transposed(left, right):
    return lax.dot_general(
        left, right, (((0,), (0,)), ((), ())), precision=HIGHEST, preferred_element_type=jnp.float32
    )


def exact_rows(left, right):
    return lax.dot_general(
        left, right, (((1,), (1,)), ((), ())), precision=HIGHEST, preferred_element_type=jnp.float32
    )


def product(left, right):
    return jnp.dot(left, right, precision=HIGHEST, preferred_element_type=jnp.float32)


def identity(rows, columns):
    down = lax.broadcasted_iota(jnp.int32, (rows, columns), 0)
    across = lax.broadcasted_iota(jnp.int32, (rows, columns), 1)
    return jnp.where(down == across, 1.0, 0.0).astype(jnp.float32)


def factor_inverse(gram):
    size = gram.shape[0]
    wide = jnp.concatenate([gram, identity(size, size)], axis=1)
    tile = (8, 2 * size)
    rows = [wide[8 * g : 8 * g + 8] for g in range(size // 8)]
    sub = lax.broadcasted_iota(jnp.int32, tile, 0)
    done = []
    low = high = total = None
    for g in range(size // 8):
        live = rows[g:]
        panel = [[jnp.broadcast_to(r[:, 8 * g + j : 8 * g + j + 1], tile) for r in live] for j in range(8)]
        scale = None
        for j in range(8):
            head = panel[j][0]
            pivot = jnp.broadcast_to(head[j : j + 1], tile)
            inverse = 1.0 / pivot
            row = jnp.broadcast_to(live[0][j : j + 1], tile)
            factors = [value * inverse for value in panel[j]]
            factors[0] = jnp.where(sub > j, factors[0], 0.0)
            for i in range(j + 1, 8):
                other = jnp.broadcast_to(head[i : i + 1], tile)
                panel[i] = [value - f * other for value, f in zip(panel[i], factors)]
            live = [value - f * row for value, f in zip(live, factors)]
            scale = pivot if scale is None else jnp.where(sub >= j, pivot, scale)
            low = pivot if low is None else jnp.minimum(low, pivot)
            high = pivot if high is None else jnp.maximum(high, pivot)
            total = pivot if total is None else total + pivot
        rows[g:] = live
        done.append(live[0] * lax.rsqrt(scale))
    return jnp.concatenate(done, axis=0)[:, size:], low, high, total


def whiten_given_kernel(gram_ref, out_ref):
    cols = gram_ref.shape[0] // 2
    first = factor_inverse(gram_ref[:cols, :cols])[0]
    lower = exact_rows(gram_ref[cols:, :cols], first)
    second = factor_inverse(gram_ref[cols:, cols:] - exact_rows(lower, lower))[0]
    out_ref[:cols, :cols] = first
    out_ref[:cols, cols:] = jnp.zeros((cols, cols), jnp.float32)
    out_ref[cols:, :cols] = -product(second, product(lower, first))
    out_ref[cols:, cols:] = second


def whiten_given(gram_matrix):
    return pl.pallas_call(
        whiten_given_kernel,
        out_shape=jax.ShapeDtypeStruct(gram_matrix.shape, jnp.float32),
        cost_estimate=pl.CostEstimate(flops=4_000_000_000, transcendentals=0, bytes_accessed=131072),
        name="whiten_given",
    )(gram_matrix)


def whiten_rest_kernel(given_ref, gram_ref, out_ref):
    cols, size = gram_ref.shape
    lower = exact_rows(gram_ref[:, : size - cols], given_ref[...])
    last = factor_inverse(gram_ref[:, size - cols :] - exact_rows(lower, lower))[0]
    out_ref[:, : size - cols] = -product(last, product(lower, given_ref[...]))
    out_ref[:, size - cols :] = last


def whiten_rest(given, gram_rows):
    return pl.pallas_call(
        whiten_rest_kernel,
        out_shape=jax.ShapeDtypeStruct(gram_rows.shape, jnp.float32),
        cost_estimate=pl.CostEstimate(flops=3_000_000_000, transcendentals=0, bytes_accessed=131072),
        name="whiten_rest",
    )(given, gram_rows)


def ritz_kernel(
    given_ref, rest_ref, raw_given_ref, raw_rest_ref, coeffs_ref, values_ref,
    whiten_ref, matrix_ref, power_ref, turned_ref, basis_ref,
):
    size, cols = turned_ref.shape
    rest = size - cols
    whiten_ref[:rest, :rest] = given_ref[...]
    whiten_ref[:rest, rest:] = jnp.zeros((rest, cols), jnp.float32)
    whiten_ref[rest:, :] = rest_ref[...]
    matrix_ref[:rest, :rest] = 0.5 * (raw_given_ref[...] + raw_given_ref[...].T)
    matrix_ref[rest:, :] = raw_rest_ref[...]
    matrix_ref[:rest, rest:] = raw_rest_ref[:, :rest].T
    power_ref[...] = product(whiten_ref[...], matrix_ref[...])
    matrix_ref[...] = exact_rows(power_ref[...], whiten_ref[...])
    matrix_ref[...] = 0.5 * (matrix_ref[...] + matrix_ref[...].T)
    power_ref[...] = product(matrix_ref[...], matrix_ref[...])
    power_ref[...] = product(power_ref[...], matrix_ref[...])

    def sweep(step_ref, count):
        basis_ref[...] = identity(size, cols)

        def turn(_, good):
            turned_ref[...] = product(step_ref[...], basis_ref[...])
            turned = turned_ref[...]
            inverse, low, high, total = factor_inverse(exact_transposed(turned, turned))
            basis_ref[...] = exact_rows(turned_ref[...], inverse)
            fine = jnp.logical_and(low > SPREAD * high, total < LARGE)
            return jnp.minimum(good, jnp.where(fine, 1.0, 0.0))

        return lax.fori_loop(0, count, turn, jnp.ones((8, 2 * cols), jnp.float32))

    good = jnp.min(sweep(power_ref, NSUB // 3))

    @pl.when(good < 0.5)
    def _():
        sweep(matrix_ref, NSUB)

    values_ref[...] = jnp.sum(
        basis_ref[...] * product(matrix_ref[...], basis_ref[...]), axis=0, keepdims=True
    )
    down = lax.broadcasted_iota(jnp.int32, (size, cols), 0)
    coeffs_ref[:, :cols] = exact_transposed(whiten_ref[...], basis_ref[...])
    coeffs_ref[:, cols:] = exact_transposed(
        whiten_ref[...], jnp.where(down >= cols, basis_ref[...], 0.0)
    )


def ritz_of(given, rest, raw_given, raw_rest):
    cols, size = rest.shape
    return pl.pallas_call(
        ritz_kernel,
        out_shape=(
            jax.ShapeDtypeStruct((size, 2 * cols), jnp.float32),
            jax.ShapeDtypeStruct((1, cols), jnp.float32),
        ),
        scratch_shapes=[
            pltpu.VMEM((size, size), jnp.float32),
            pltpu.VMEM((size, size), jnp.float32),
            pltpu.VMEM((size, size), jnp.float32),
            pltpu.VMEM((size, cols), jnp.float32),
            pltpu.VMEM((size, cols), jnp.float32),
        ],
        cost_estimate=pl.CostEstimate(flops=10_000_000_000, transcendentals=0, bytes_accessed=524288),
        name="ritz",
    )(given, rest, raw_given, raw_rest)


def rounded(value):
    return lax.reduce_precision(value, exponent_bits=8, mantissa_bits=7)


def swap(value, axis, step):
    return lax.ppermute(value, axis, [(i, i ^ step) for i in range(lax.axis_size(axis))])


def steps_of(axis):
    size = lax.axis_size(axis)
    if size & (size - 1):
        raise ValueError(axis)
    return [1 << bit for bit in range(size.bit_length() - 1)]


def reduce_all(value, axis):
    size = lax.axis_size(axis)
    if size == 4:
        near, far, across = (swap(value, axis, step) for step in (1, 2, 3))
        return (value + near) + (far + across)
    for step in steps_of(axis):
        value = value + swap(value, axis, step)
    return value


def side_of(axis, step):
    return (lax.axis_index(axis) // step) % 2


def reduce_halves(value, axis):
    for step in steps_of(axis):
        half = value.shape[1] // 2
        side = side_of(axis, step)
        kept = lax.dynamic_slice_in_dim(value, side * half, half, 1)
        sent = lax.dynamic_slice_in_dim(value, (1 - side) * half, half, 1)
        value = kept + swap(sent, axis, step)
    return value


def own_part(value, axis):
    for step in steps_of(axis):
        half = value.shape[1] // 2
        value = lax.dynamic_slice_in_dim(value, side_of(axis, step) * half, half, 1)
    return value


def gather_halves(value, axis):
    for step in reversed(steps_of(axis)):
        other = swap(value, axis, step)
        first = side_of(axis, step) == 0
        value = jnp.concatenate([jnp.where(first, value, other), jnp.where(first, other, value)], axis=1)
    return value


def probe_of(rows_b, slab_part):
    return lax.dot_general(
        rows_b, slab_part, (((1,), (1,)), ((), ())), preferred_element_type=jnp.float32
    )


def probe_of_exact(rows_b, rows):
    total = None
    for _ in range(3):
        part = rounded(rows)
        rows = rows - part
        term = probe_of(rows_b, part.astype(jnp.bfloat16))
        total = term if total is None else total + term
    return total


def reordered(value, chunks):
    rows, width = value.shape
    devices = lax.axis_size("token")
    piece = width // (chunks * devices)
    pieces = [
        [value[:, piece * (chunks * d + c) : piece * (chunks * d + c) + piece] for d in range(devices)]
        for c in range(chunks)
    ]
    return jnp.concatenate([p for line in pieces for p in line], axis=1)


def after(value, *earlier):
    return lax.optimization_barrier((value, *earlier))[0]


def local(hidden_slab, current_block, direction):
    tok_rows, half_width = hidden_slab.shape
    cols = current_block.shape[1]
    feat_total = half_width * lax.axis_size("layer") * lax.axis_size("fhalf")
    token_total = tok_rows * lax.axis_size("token")
    ritz_scale = 1.0 / (token_total * feat_total)
    x_rows = current_block.T
    d_rows = direction.T
    chunk = half_width // CHUNKS
    starts = [chunk * c for c in range(CHUNKS)]
    slabs = [hidden_slab[:, at : at + chunk] for at in starts]
    given_b = jnp.concatenate([x_rows, d_rows], axis=0).astype(jnp.bfloat16)
    given_part = probe_of(given_b, hidden_slab)
    x_probe = reduce_all(reduce_halves(given_part[:cols], "fhalf"), "layer")
    x_probe_b = rounded(x_probe)
    block_probe = gather_halves(x_probe_b.astype(jnp.bfloat16), "fhalf")
    image_parts = [jnp.dot(block_probe, slab, preferred_element_type=jnp.float32) for slab in slabs]
    late_probe = after(block_probe, image_parts[-1])
    ritz_block = reduce_all(probe_of(late_probe, late_probe), "token") * ritz_scale
    images = [reduce_halves(part, "token") for part in image_parts]
    residuals = [
        image / token_total
        - exact_transposed(ritz_block, own_part(x_rows[:, at : at + chunk], "token"))
        for image, at in zip(images, starts)
    ]
    highs = [rounded(residual) for residual in residuals]
    search = [gather_halves(high.astype(jnp.bfloat16), "token") for high in highs]
    x_late, d_late = lax.optimization_barrier((x_rows, d_rows, image_parts[-1]))[:2]
    gram_given = exact_rows(
        jnp.concatenate([x_late, d_late], axis=0), jnp.concatenate([x_late, d_late], axis=0)
    )
    joined = jnp.concatenate([given_part[cols:], gram_given[:cols], gram_given[cols:]], axis=1)
    joined = lax.psum(joined, ("layer", "fhalf"))
    d_probe = joined[:, :tok_rows]
    gram_given = jnp.concatenate(
        [joined[:, tok_rows : tok_rows + 2 * cols], joined[:, tok_rows + 2 * cols :]], axis=0
    )
    given_inverse = whiten_given(gram_given / feat_total)
    d_own = own_part(d_probe, "fhalf")
    given_probe = jnp.concatenate([x_probe, d_own], axis=0)
    given_probe_b = jnp.concatenate([x_probe_b, rounded(d_own)], axis=0)
    r_part = sum(probe_of(rows, slab) for rows, slab in zip(search, slabs))
    search_rows = jnp.concatenate(search, axis=1)
    gram_rest = jnp.concatenate(
        [probe_of_exact(search_rows, x_rows), probe_of_exact(search_rows, d_rows),
         probe_of(search_rows, search_rows)], axis=1
    )
    r_half = reduce_halves(r_part, "fhalf")
    gram_rest = reduce_all(gram_rest, "fhalf")
    r_joined = jnp.concatenate([r_half, gram_rest], axis=1)
    raw_given = exact_rows(*lax.optimization_barrier((given_probe, given_probe_b, r_joined))[:2])
    r_joined = reduce_all(r_joined, "layer")
    r_probe = r_joined[:, : r_half.shape[1]]
    gram_rest = r_joined[:, r_half.shape[1] :]
    raw_given = reduce_all(reduce_all(raw_given, "fhalf"), "token") * ritz_scale
    r_probe_b = rounded(r_probe)
    raw_rest = jnp.concatenate(
        [
            0.5 * (exact_rows(r_probe, given_probe_b) + exact_rows(r_probe_b, given_probe)),
            exact_rows(r_probe, r_probe_b),
        ],
        axis=1,
    )
    raw_rest = reduce_all(raw_rest, "fhalf")
    rest_inverse = whiten_rest(given_inverse, after(gram_rest, raw_rest) / feat_total)
    residual_lo = jnp.concatenate(
        [(residual - high).astype(jnp.bfloat16) for residual, high in zip(residuals, highs)], axis=1
    )
    residual_lo = gather_halves(after(residual_lo, raw_rest), "token")
    raw_rest = reduce_all(raw_rest, "token") * ritz_scale
    all_coeffs, ritz_values = ritz_of(given_inverse, rest_inverse, raw_given, raw_rest)
    residual_rows = search_rows.astype(jnp.float32) + reordered(residual_lo, CHUNKS).astype(jnp.float32)
    search_basis = jnp.concatenate([x_rows, d_rows, residual_rows], axis=0)
    new_block = exact_transposed(all_coeffs[:, :cols], search_basis)
    new_direction = exact_transposed(all_coeffs[:, cols:], search_basis)
    return (new_block.T, new_direction.T, ritz_values[0])


def solution(mesh):
    return jax.shard_map(
        local,
        mesh=mesh,
        in_specs=(
            P("token", ("layer", "fhalf")),
            P(("layer", "fhalf"), None),
            P(("layer", "fhalf"), None),
        ),
        out_specs=(P(("layer", "fhalf"), None), P(("layer", "fhalf"), None), P()),
        check_vma=False,
    )
```

```python
import jax
import jax.numpy as jnp
from jax import lax
from jax.experimental import pallas as pl
from jax.experimental.pallas import tpu as pltpu
from jax.sharding import PartitionSpec as P

NSUB = 6
CHUNKS = 2
SPREAD = 1e-4
LARGE = 1e30
HIGHEST = lax.Precision.HIGHEST


def exact_transposed(left, right):
    return lax.dot_general(
        left, right, (((0,), (0,)), ((), ())), precision=HIGHEST, preferred_element_type=jnp.float32
    )


def exact_rows(left, right):
    return lax.dot_general(
        left, right, (((1,), (1,)), ((), ())), precision=HIGHEST, preferred_element_type=jnp.float32
    )


def product(left, right):
    return jnp.dot(left, right, precision=HIGHEST, preferred_element_type=jnp.float32)


def identity(rows, columns):
    down = lax.broadcasted_iota(jnp.int32, (rows, columns), 0)
    across = lax.broadcasted_iota(jnp.int32, (rows, columns), 1)
    return jnp.where(down == across, 1.0, 0.0).astype(jnp.float32)


def factor_inverse(gram):
    size = gram.shape[0]
    wide = jnp.concatenate([gram, identity(size, size)], axis=1)
    tile = (8, 2 * size)
    rows = [wide[8 * g : 8 * g + 8] for g in range(size // 8)]
    sub = lax.broadcasted_iota(jnp.int32, tile, 0)
    done = []
    low = high = total = None
    for g in range(size // 8):
        live = rows[g:]
        panel = [[jnp.broadcast_to(r[:, 8 * g + j : 8 * g + j + 1], tile) for r in live] for j in range(8)]
        scale = None
        for j in range(8):
            head = panel[j][0]
            pivot = jnp.broadcast_to(head[j : j + 1], tile)
            inverse = 1.0 / pivot
            row = jnp.broadcast_to(live[0][j : j + 1], tile)
            factors = [value * inverse for value in panel[j]]
            factors[0] = jnp.where(sub > j, factors[0], 0.0)
            for i in range(j + 1, 8):
                other = jnp.broadcast_to(head[i : i + 1], tile)
                panel[i] = [value - f * other for value, f in zip(panel[i], factors)]
            live = [value - f * row for value, f in zip(live, factors)]
            scale = pivot if scale is None else jnp.where(sub >= j, pivot, scale)
            low = pivot if low is None else jnp.minimum(low, pivot)
            high = pivot if high is None else jnp.maximum(high, pivot)
            total = pivot if total is None else total + pivot
        rows[g:] = live
        done.append(live[0] * lax.rsqrt(scale))
    return jnp.concatenate(done, axis=0)[:, size:], low, high, total


def whiten_given_kernel(gram_ref, out_ref):
    cols = gram_ref.shape[0] // 2
    first = factor_inverse(gram_ref[:cols, :cols])[0]
    lower = exact_rows(gram_ref[cols:, :cols], first)
    second = factor_inverse(gram_ref[cols:, cols:] - exact_rows(lower, lower))[0]
    out_ref[:cols, :cols] = first
    out_ref[:cols, cols:] = jnp.zeros((cols, cols), jnp.float32)
    out_ref[cols:, :cols] = -product(second, product(lower, first))
    out_ref[cols:, cols:] = second


def whiten_given(gram_matrix):
    return pl.pallas_call(
        whiten_given_kernel,
        out_shape=jax.ShapeDtypeStruct(gram_matrix.shape, jnp.float32),
        cost_estimate=pl.CostEstimate(flops=4_000_000_000, transcendentals=0, bytes_accessed=131072),
        name="whiten_given",
    )(gram_matrix)


def whiten_rest_kernel(given_ref, gram_ref, out_ref):
    cols, size = gram_ref.shape
    lower = exact_rows(gram_ref[:, : size - cols], given_ref[...])
    last = factor_inverse(gram_ref[:, size - cols :] - exact_rows(lower, lower))[0]
    out_ref[:, : size - cols] = -product(last, product(lower, given_ref[...]))
    out_ref[:, size - cols :] = last


def whiten_rest(given, gram_rows):
    return pl.pallas_call(
        whiten_rest_kernel,
        out_shape=jax.ShapeDtypeStruct(gram_rows.shape, jnp.float32),
        cost_estimate=pl.CostEstimate(flops=3_000_000_000, transcendentals=0, bytes_accessed=131072),
        name="whiten_rest",
    )(given, gram_rows)


def ritz_kernel(
    given_ref, rest_ref, raw_given_ref, raw_rest_ref, coeffs_ref, values_ref,
    whiten_ref, matrix_ref, power_ref, turned_ref, basis_ref,
):
    size, cols = turned_ref.shape
    rest = size - cols
    whiten_ref[:rest, :rest] = given_ref[...]
    whiten_ref[:rest, rest:] = jnp.zeros((rest, cols), jnp.float32)
    whiten_ref[rest:, :] = rest_ref[...]
    matrix_ref[:rest, :rest] = 0.5 * (raw_given_ref[...] + raw_given_ref[...].T)
    matrix_ref[rest:, :] = raw_rest_ref[...]
    matrix_ref[:rest, rest:] = raw_rest_ref[:, :rest].T
    power_ref[...] = product(whiten_ref[...], matrix_ref[...])
    matrix_ref[...] = exact_rows(power_ref[...], whiten_ref[...])
    matrix_ref[...] = 0.5 * (matrix_ref[...] + matrix_ref[...].T)
    power_ref[...] = product(matrix_ref[...], matrix_ref[...])
    power_ref[...] = product(power_ref[...], matrix_ref[...])

    def sweep(step_ref, count):
        def turn(number, good):
            @pl.when(number == 0)
            def _():
                turned_ref[...] = step_ref[:, :cols]

            @pl.when(number > 0)
            def _():
                turned_ref[...] = product(step_ref[...], basis_ref[...])

            turned = turned_ref[...]
            inverse, low, high, total = factor_inverse(exact_transposed(turned, turned))
            basis_ref[...] = exact_rows(turned_ref[...], inverse)
            fine = jnp.logical_and(low > SPREAD * high, total < LARGE)
            return jnp.minimum(good, jnp.where(fine, 1.0, 0.0))

        return lax.fori_loop(0, count, turn, jnp.ones((8, 2 * cols), jnp.float32))

    good = jnp.min(sweep(power_ref, NSUB // 3))

    @pl.when(good < 0.5)
    def _():
        sweep(matrix_ref, NSUB)

    values_ref[...] = jnp.sum(
        basis_ref[...] * product(matrix_ref[...], basis_ref[...]), axis=0, keepdims=True
    )
    down = lax.broadcasted_iota(jnp.int32, (size, cols), 0)
    power_ref[:, :cols] = basis_ref[...]
    power_ref[:, cols : 2 * cols] = jnp.where(down >= cols, basis_ref[...], 0.0)
    coeffs_ref[...] = exact_transposed(whiten_ref[...], power_ref[:, : 2 * cols])


def ritz_of(given, rest, raw_given, raw_rest):
    cols, size = rest.shape
    return pl.pallas_call(
        ritz_kernel,
        out_shape=(
            jax.ShapeDtypeStruct((size, 2 * cols), jnp.float32),
            jax.ShapeDtypeStruct((1, cols), jnp.float32),
        ),
        scratch_shapes=[
            pltpu.VMEM((size, size), jnp.float32),
            pltpu.VMEM((size, size), jnp.float32),
            pltpu.VMEM((size, size), jnp.float32),
            pltpu.VMEM((size, cols), jnp.float32),
            pltpu.VMEM((size, cols), jnp.float32),
        ],
        cost_estimate=pl.CostEstimate(flops=10_000_000_000, transcendentals=0, bytes_accessed=524288),
        name="ritz",
    )(given, rest, raw_given, raw_rest)


def rounded(value):
    return lax.reduce_precision(value, exponent_bits=8, mantissa_bits=7)


def moved(coeffs, rows):
    return lax.dot_general(
        coeffs,
        rows,
        (((0,), (0,)), ((), ())),
        precision=lax.Precision.HIGH,
        preferred_element_type=jnp.float32,
    )


def swap(value, axis, step):
    return lax.ppermute(value, axis, [(i, i ^ step) for i in range(lax.axis_size(axis))])


def steps_of(axis):
    size = lax.axis_size(axis)
    if size & (size - 1):
        raise ValueError(axis)
    return [1 << bit for bit in range(size.bit_length() - 1)]


def reduce_all(value, axis):
    size = lax.axis_size(axis)
    if size == 4:
        near, far, across = (swap(value, axis, step) for step in (1, 2, 3))
        return (value + near) + (far + across)
    for step in steps_of(axis):
        value = value + swap(value, axis, step)
    return value


def side_of(axis, step):
    return (lax.axis_index(axis) // step) % 2


def sent_half(value, axis, step):
    half = value.shape[1] // 2
    return lax.dynamic_slice_in_dim(value, (1 - side_of(axis, step)) * half, half, 1)


def kept_half(value, axis, step):
    half = value.shape[1] // 2
    return lax.dynamic_slice_in_dim(value, side_of(axis, step) * half, half, 1)


def reduce_halves(value, axis):
    for step in steps_of(axis):
        value = kept_half(value, axis, step) + swap(sent_half(value, axis, step), axis, step)
    return value


def own_part(value, axis):
    for step in steps_of(axis):
        value = kept_half(value, axis, step)
    return value


def joined_halves(value, axis, step):
    other = swap(value, axis, step)
    first = side_of(axis, step) == 0
    return jnp.concatenate([jnp.where(first, value, other), jnp.where(first, other, value)], axis=1)


def gather_halves(value, axis):
    for step in reversed(steps_of(axis)):
        value = joined_halves(value, axis, step)
    return value


def probe_of(rows_b, slab_part):
    return lax.dot_general(
        rows_b, slab_part, (((1,), (1,)), ((), ())), preferred_element_type=jnp.float32
    )


def reordered(value, chunks):
    rows, width = value.shape
    devices = lax.axis_size("token")
    piece = width // (chunks * devices)
    pieces = [
        [value[:, piece * (chunks * d + c) : piece * (chunks * d + c) + piece] for d in range(devices)]
        for c in range(chunks)
    ]
    return jnp.concatenate([p for line in pieces for p in line], axis=1)


def after(value, *earlier):
    return lax.optimization_barrier((value, *earlier))[0]


def local(hidden_slab, current_block, direction):
    tok_rows, half_width = hidden_slab.shape
    cols = current_block.shape[1]
    feat_total = half_width * lax.axis_size("layer") * lax.axis_size("fhalf")
    token_total = tok_rows * lax.axis_size("token")
    ritz_scale = 1.0 / (token_total * feat_total)
    x_rows = current_block.T
    d_rows = direction.T
    chunk = half_width // CHUNKS
    starts = [chunk * c for c in range(CHUNKS)]
    slabs = [hidden_slab[:, at : at + chunk] for at in starts]
    given_rows = jnp.concatenate([x_rows, d_rows], axis=0)
    given_hi = rounded(given_rows)
    given_b = given_hi.astype(jnp.bfloat16)
    given_lo = (given_rows - given_hi).astype(jnp.bfloat16)
    given_part = probe_of(jnp.concatenate([given_b, given_lo[:cols]], axis=0), hidden_slab)
    x_probe = reduce_all(reduce_halves(given_part[:cols], "fhalf"), "layer")
    x_probe_b = rounded(x_probe)
    block_probe = gather_halves(x_probe_b.astype(jnp.bfloat16), "fhalf")
    token_steps = steps_of("token")
    parts, sents = [], []
    for slab in slabs:
        probe = after(block_probe, sents[-1]) if sents else block_probe
        part = jnp.dot(probe, slab, preferred_element_type=jnp.float32)
        sent = sent_half(part, "token", token_steps[0])
        if not parts:
            ritz_block = probe_of(block_probe, block_probe)
            sent = jnp.concatenate([sent, ritz_block], axis=1)
        parts.append(part)
        sents.append(sent)
    for number, step in enumerate(token_steps):
        images = []
        for c in range(CHUNKS):
            got = swap(sents[c], "token", step)
            if c == 0:
                ritz_block = ritz_block + got[:, got.shape[1] - cols :]
                got = got[:, : got.shape[1] - cols]
            images.append(kept_half(parts[c], "token", step) + got)
        parts = images
        if number + 1 < len(token_steps):
            sents = [sent_half(part, "token", token_steps[number + 1]) for part in parts]
            sents[0] = jnp.concatenate([sents[0], ritz_block], axis=1)
        if number == 0:
            d_part, late_rows = lax.optimization_barrier((given_part[cols:], given_rows, sents[0]))[:2]
            gram_given = exact_rows(late_rows, late_rows)
            gram_given = jnp.concatenate([gram_given[:cols], gram_given[cols:]], axis=1)
            near = steps_of("fhalf")[0]
            joined_sent, joined_kept = (
                jnp.concatenate([half[:cols], half[cols:], gram_given], axis=1)
                for half in (sent_half(d_part, "fhalf", near), kept_half(d_part, "fhalf", near))
            )
            joined = joined_kept + swap(joined_sent, "fhalf", near)
            joined = after(joined, *sents)
    ritz_block = ritz_block * ritz_scale
    residuals = [
        image / token_total
        - exact_transposed(ritz_block, own_part(x_rows[:, at : at + chunk], "token"))
        for image, at in zip(images, starts)
    ]
    highs = [rounded(residual) for residual in residuals]
    high_b = [high.astype(jnp.bfloat16) for high in highs]
    search = [gather_halves(high, "token") for high in high_b]
    joined = reduce_all(joined, "layer")
    r_part = sum(probe_of(rows, slab) for rows, slab in zip(search, slabs))
    search_rows = jnp.concatenate(search, axis=1)
    gram_rest = jnp.concatenate(
        [
            probe_of(search_rows, given_b) + probe_of(search_rows, given_lo),
            probe_of(search_rows, search_rows),
        ],
        axis=1,
    )
    step = steps_of("fhalf")[0]
    r_sent = jnp.concatenate([sent_half(r_part, "fhalf", step), gram_rest], axis=1)
    r_kept = jnp.concatenate([kept_half(r_part, "fhalf", step), gram_rest], axis=1)
    r_joined = r_kept + swap(r_sent, "fhalf", step)
    joined = after(joined, r_joined)
    half_rows = tok_rows // 2
    d_probe = joined[:, :half_rows]
    x_full = x_probe + joined[:, half_rows : 2 * half_rows]
    gram_given = joined[:, 2 * half_rows :]
    gram_given = jnp.concatenate([gram_given[:, : 2 * cols], gram_given[:, 2 * cols :]], axis=0)
    given_inverse = whiten_given(gram_given / feat_total)
    given_probe = jnp.concatenate([x_full, d_probe], axis=0)
    given_probe_b = jnp.concatenate([x_probe_b, rounded(d_probe)], axis=0)
    raw_given = exact_rows(given_probe, given_probe_b)
    raw_given = jnp.concatenate([raw_given[:cols], raw_given[cols:]], axis=1)
    residual_lo = jnp.concatenate(
        [(residual - high).astype(jnp.bfloat16) for residual, high in zip(residuals, highs)], axis=1
    )
    residual_lo = after(residual_lo, r_part)
    r_joined = reduce_all(r_joined, "layer")
    r_probe = r_joined[:, :half_rows]
    gram_rest = r_joined[:, half_rows:]
    r_probe_b = rounded(r_probe)
    raw = jnp.concatenate(
        [
            0.5 * (exact_rows(r_probe, given_probe_b) + exact_rows(r_probe_b, given_probe)),
            exact_rows(r_probe, r_probe_b),
            raw_given,
        ],
        axis=1,
    )
    near = steps_of("fhalf")[0]
    side = side_of("fhalf", near)
    raw = lax.dynamic_slice_in_dim(raw, side * (cols // 2), cols // 2, 0) + swap(
        lax.dynamic_slice_in_dim(raw, (1 - side) * (cols // 2), cols // 2, 0), "fhalf", near
    )
    rest_inverse = whiten_rest(given_inverse, after(gram_rest, raw) / feat_total)
    raw = reduce_all(raw, "token") * ritz_scale
    other = swap(raw, "fhalf", near)
    raw = jnp.concatenate(
        [jnp.where(side == 0, raw, other), jnp.where(side == 0, other, raw)], axis=0
    )
    raw_rest = raw[:, : 3 * cols]
    raw_given = jnp.concatenate([raw[:, 3 * cols : 5 * cols], raw[:, 5 * cols :]], axis=0)
    all_coeffs, ritz_values = ritz_of(given_inverse, rest_inverse, raw_given, raw_rest)
    for step in reversed(token_steps):
        if step == token_steps[0]:
            residual_lo = after(residual_lo, raw)
        residual_lo = joined_halves(residual_lo, "token", step)
    residual_rows = search_rows.astype(jnp.float32) + reordered(residual_lo, CHUNKS).astype(jnp.float32)
    search_basis = jnp.concatenate([x_rows, d_rows, residual_rows], axis=0)
    new_block = moved(all_coeffs[:, :cols], search_basis)
    new_direction = moved(all_coeffs[:, cols:], search_basis)
    return (new_block.T, new_direction.T, ritz_values[0])


def solution(mesh):
    return jax.shard_map(
        local,
        mesh=mesh,
        in_specs=(
            P("token", ("layer", "fhalf")),
            P(("layer", "fhalf"), None),
            P(("layer", "fhalf"), None),
        ),
        out_specs=(P(("layer", "fhalf"), None), P(("layer", "fhalf"), None), P()),
        check_vma=False,
    )
```

```python
import jax
import jax.numpy as jnp
from jax import lax
from jax.experimental import pallas as pl
from jax.experimental.pallas import tpu as pltpu
from jax.sharding import PartitionSpec as P

NSUB = 6
CHUNKS = 2
SPREAD = 1e-4
LARGE = 1e30
HIGHEST = lax.Precision.HIGHEST


def exact_transposed(left, right):
    return lax.dot_general(
        left, right, (((0,), (0,)), ((), ())), precision=HIGHEST, preferred_element_type=jnp.float32
    )


def exact_rows(left, right):
    return lax.dot_general(
        left, right, (((1,), (1,)), ((), ())), precision=HIGHEST, preferred_element_type=jnp.float32
    )


def product(left, right):
    return jnp.dot(left, right, precision=HIGHEST, preferred_element_type=jnp.float32)


def identity(rows, columns):
    down = lax.broadcasted_iota(jnp.int32, (rows, columns), 0)
    across = lax.broadcasted_iota(jnp.int32, (rows, columns), 1)
    return jnp.where(down == across, 1.0, 0.0).astype(jnp.float32)


def factor_inverse(gram):
    size = gram.shape[0]
    wide = jnp.concatenate([gram, identity(size, size)], axis=1)
    tile = (8, 2 * size)
    rows = [wide[8 * g : 8 * g + 8] for g in range(size // 8)]
    sub = lax.broadcasted_iota(jnp.int32, tile, 0)
    done = []
    low = high = total = None
    for g in range(size // 8):
        live = rows[g:]
        panel = [[jnp.broadcast_to(r[:, 8 * g + j : 8 * g + j + 1], tile) for r in live] for j in range(8)]
        scale = None
        for j in range(8):
            head = panel[j][0]
            pivot = jnp.broadcast_to(head[j : j + 1], tile)
            inverse = 1.0 / pivot
            row = jnp.broadcast_to(live[0][j : j + 1], tile)
            factors = [value * inverse for value in panel[j]]
            factors[0] = jnp.where(sub > j, factors[0], 0.0)
            for i in range(j + 1, 8):
                other = jnp.broadcast_to(head[i : i + 1], tile)
                panel[i] = [value - f * other for value, f in zip(panel[i], factors)]
            live = [value - f * row for value, f in zip(live, factors)]
            scale = pivot if scale is None else jnp.where(sub >= j, pivot, scale)
            low = pivot if low is None else jnp.minimum(low, pivot)
            high = pivot if high is None else jnp.maximum(high, pivot)
            total = pivot if total is None else total + pivot
        rows[g:] = live
        done.append(live[0] * lax.rsqrt(scale))
    return jnp.concatenate(done, axis=0)[:, size:], low, high, total


def whiten_given_kernel(gram_ref, out_ref):
    cols = gram_ref.shape[0] // 2
    first = factor_inverse(gram_ref[:cols, :cols])[0]
    lower = exact_rows(gram_ref[cols:, :cols], first)
    second = factor_inverse(gram_ref[cols:, cols:] - exact_rows(lower, lower))[0]
    out_ref[:cols, :cols] = first
    out_ref[:cols, cols:] = jnp.zeros((cols, cols), jnp.float32)
    out_ref[cols:, :cols] = -product(second, product(lower, first))
    out_ref[cols:, cols:] = second


def whiten_given(gram_matrix):
    return pl.pallas_call(
        whiten_given_kernel,
        out_shape=jax.ShapeDtypeStruct(gram_matrix.shape, jnp.float32),
        cost_estimate=pl.CostEstimate(flops=4_000_000_000, transcendentals=0, bytes_accessed=131072),
        name="whiten_given",
    )(gram_matrix)


def whiten_rest_kernel(given_ref, gram_ref, out_ref):
    cols, size = gram_ref.shape
    lower = exact_rows(gram_ref[:, : size - cols], given_ref[...])
    last = factor_inverse(gram_ref[:, size - cols :] - exact_rows(lower, lower))[0]
    out_ref[:, : size - cols] = -product(last, product(lower, given_ref[...]))
    out_ref[:, size - cols :] = last


def whiten_rest(given, gram_rows):
    return pl.pallas_call(
        whiten_rest_kernel,
        out_shape=jax.ShapeDtypeStruct(gram_rows.shape, jnp.float32),
        cost_estimate=pl.CostEstimate(flops=3_000_000_000, transcendentals=0, bytes_accessed=131072),
        name="whiten_rest",
    )(given, gram_rows)


def ritz_kernel(
    given_ref, rest_ref, raw_given_ref, raw_rest_ref, coeffs_ref, values_ref,
    whiten_ref, matrix_ref, power_ref, turned_ref, basis_ref,
):
    size, cols = turned_ref.shape
    rest = size - cols
    whiten_ref[:rest, :rest] = given_ref[...]
    whiten_ref[:rest, rest:] = jnp.zeros((rest, cols), jnp.float32)
    whiten_ref[rest:, :] = rest_ref[...]
    matrix_ref[:rest, :rest] = 0.5 * (raw_given_ref[...] + raw_given_ref[...].T)
    matrix_ref[rest:, :] = raw_rest_ref[...]
    matrix_ref[:rest, rest:] = raw_rest_ref[:, :rest].T
    power_ref[...] = product(whiten_ref[...], matrix_ref[...])
    matrix_ref[...] = exact_rows(power_ref[...], whiten_ref[...])
    matrix_ref[...] = 0.5 * (matrix_ref[...] + matrix_ref[...].T)
    power_ref[...] = product(matrix_ref[...], matrix_ref[...])
    power_ref[...] = product(power_ref[...], matrix_ref[...])

    def sweep(step_ref, count):
        def turn(number, good):
            @pl.when(number == 0)
            def _():
                turned_ref[...] = step_ref[:, :cols]

            @pl.when(number > 0)
            def _():
                turned_ref[...] = product(step_ref[...], basis_ref[...])

            turned = turned_ref[...]
            inverse, low, high, total = factor_inverse(exact_transposed(turned, turned))
            basis_ref[...] = exact_rows(turned_ref[...], inverse)
            fine = jnp.logical_and(low > SPREAD * high, total < LARGE)
            return jnp.minimum(good, jnp.where(fine, 1.0, 0.0))

        return lax.fori_loop(0, count, turn, jnp.ones((8, 2 * cols), jnp.float32))

    good = jnp.min(sweep(power_ref, NSUB // 3))

    @pl.when(good < 0.5)
    def _():
        sweep(matrix_ref, NSUB)

    values_ref[...] = jnp.sum(
        basis_ref[...] * product(matrix_ref[...], basis_ref[...]), axis=0, keepdims=True
    )
    down = lax.broadcasted_iota(jnp.int32, (size, cols), 0)
    power_ref[:, :cols] = basis_ref[...]
    power_ref[:, cols : 2 * cols] = jnp.where(down >= cols, basis_ref[...], 0.0)
    coeffs_ref[...] = exact_transposed(whiten_ref[...], power_ref[:, : 2 * cols])


def ritz_of(given, rest, raw_given, raw_rest):
    cols, size = rest.shape
    return pl.pallas_call(
        ritz_kernel,
        out_shape=(
            jax.ShapeDtypeStruct((size, 2 * cols), jnp.float32),
            jax.ShapeDtypeStruct((1, cols), jnp.float32),
        ),
        scratch_shapes=[
            pltpu.VMEM((size, size), jnp.float32),
            pltpu.VMEM((size, size), jnp.float32),
            pltpu.VMEM((size, size), jnp.float32),
            pltpu.VMEM((size, cols), jnp.float32),
            pltpu.VMEM((size, cols), jnp.float32),
        ],
        cost_estimate=pl.CostEstimate(flops=10_000_000_000, transcendentals=0, bytes_accessed=524288),
        name="ritz",
    )(given, rest, raw_given, raw_rest)


def rounded(value):
    return lax.reduce_precision(value, exponent_bits=8, mantissa_bits=7)


def moved(coeffs, rows):
    return lax.dot_general(
        coeffs,
        rows,
        (((0,), (0,)), ((), ())),
        precision=lax.Precision.HIGH,
        preferred_element_type=jnp.float32,
    )


def swap(value, axis, step):
    return lax.ppermute(value, axis, [(i, i ^ step) for i in range(lax.axis_size(axis))])


def steps_of(axis):
    size = lax.axis_size(axis)
    if size & (size - 1):
        raise ValueError(axis)
    return [1 << bit for bit in range(size.bit_length() - 1)]


def reduce_all(value, axis):
    size = lax.axis_size(axis)
    if size == 4:
        near, far, across = (swap(value, axis, step) for step in (1, 2, 3))
        return (value + near) + (far + across)
    for step in steps_of(axis):
        value = value + swap(value, axis, step)
    return value


def side_of(axis, step):
    return (lax.axis_index(axis) // step) % 2


def sent_half(value, axis, step):
    half = value.shape[1] // 2
    return lax.dynamic_slice_in_dim(value, (1 - side_of(axis, step)) * half, half, 1)


def kept_half(value, axis, step):
    half = value.shape[1] // 2
    return lax.dynamic_slice_in_dim(value, side_of(axis, step) * half, half, 1)


def reduce_halves(value, axis):
    for step in steps_of(axis):
        value = kept_half(value, axis, step) + swap(sent_half(value, axis, step), axis, step)
    return value


def own_part(value, axis):
    for step in steps_of(axis):
        value = kept_half(value, axis, step)
    return value


def joined_halves(value, axis, step):
    other = swap(value, axis, step)
    first = side_of(axis, step) == 0
    return jnp.concatenate([jnp.where(first, value, other), jnp.where(first, other, value)], axis=1)


def gather_halves(value, axis):
    for step in reversed(steps_of(axis)):
        value = joined_halves(value, axis, step)
    return value


def probe_of(rows_b, slab_part):
    return lax.dot_general(
        rows_b, slab_part, (((1,), (1,)), ((), ())), preferred_element_type=jnp.float32
    )


def reordered(value, chunks):
    rows, width = value.shape
    devices = lax.axis_size("token")
    piece = width // (chunks * devices)
    pieces = [
        [value[:, piece * (chunks * d + c) : piece * (chunks * d + c) + piece] for d in range(devices)]
        for c in range(chunks)
    ]
    return jnp.concatenate([p for line in pieces for p in line], axis=1)


def after(value, *earlier):
    return lax.optimization_barrier((value, *earlier))[0]


def local(hidden_slab, current_block, direction):
    tok_rows, half_width = hidden_slab.shape
    cols = current_block.shape[1]
    feat_total = half_width * lax.axis_size("layer") * lax.axis_size("fhalf")
    token_total = tok_rows * lax.axis_size("token")
    ritz_scale = 1.0 / (token_total * feat_total)
    x_rows = current_block.T
    d_rows = direction.T
    chunk = half_width // CHUNKS
    starts = [chunk * c for c in range(CHUNKS)]
    slabs = [hidden_slab[:, at : at + chunk] for at in starts]
    given_rows = jnp.concatenate([x_rows, d_rows], axis=0)
    given_hi = rounded(given_rows)
    given_b = given_hi.astype(jnp.bfloat16)
    given_lo = (given_rows - given_hi).astype(jnp.bfloat16)
    given_part = probe_of(jnp.concatenate([given_b, given_lo[:cols]], axis=0), hidden_slab)
    x_probe = reduce_all(reduce_halves(given_part[:cols], "fhalf"), "layer")
    x_probe_b = rounded(x_probe)
    block_probe = gather_halves(x_probe_b.astype(jnp.bfloat16), "fhalf")
    token_steps = steps_of("token")
    parts, sents = [], []
    for slab in slabs:
        probe = after(block_probe, sents[-1]) if sents else block_probe
        part = jnp.dot(probe, slab, preferred_element_type=jnp.float32)
        sent = sent_half(part, "token", token_steps[0])
        if not parts:
            ritz_block = probe_of(block_probe, block_probe)
            sent = jnp.concatenate([sent, ritz_block], axis=1)
        parts.append(part)
        sents.append(sent)
    for number, step in enumerate(token_steps):
        images = []
        for c in range(CHUNKS):
            got = swap(sents[c], "token", step)
            if c == 0:
                ritz_block = ritz_block + got[:, got.shape[1] - cols :]
                got = got[:, : got.shape[1] - cols]
            images.append(kept_half(parts[c], "token", step) + got)
        parts = images
        if number + 1 < len(token_steps):
            sents = [sent_half(part, "token", token_steps[number + 1]) for part in parts]
            sents[0] = jnp.concatenate([sents[0], ritz_block], axis=1)
        if number == 0:
            d_part, late_rows = lax.optimization_barrier((given_part[cols:], given_rows, sents[0]))[:2]
            gram_given = exact_rows(late_rows, late_rows)
            gram_given = jnp.concatenate([gram_given[:cols], gram_given[cols:]], axis=1)
            near = steps_of("fhalf")[0]
            joined_sent, joined_kept = (
                jnp.concatenate([half[:cols], half[cols:], gram_given], axis=1)
                for half in (sent_half(d_part, "fhalf", near), kept_half(d_part, "fhalf", near))
            )
            joined = joined_kept + swap(joined_sent, "fhalf", near)
            joined = after(joined, *sents)
    ritz_block = ritz_block * ritz_scale
    residuals = [
        image / token_total
        - exact_transposed(ritz_block, own_part(x_rows[:, at : at + chunk], "token"))
        for image, at in zip(images, starts)
    ]
    highs = [rounded(residual) for residual in residuals]
    high_b = [high.astype(jnp.bfloat16) for high in highs]
    search = [gather_halves(high, "token") for high in high_b]
    joined = reduce_all(joined, "layer")
    r_part = sum(probe_of(rows, slab) for rows, slab in zip(search, slabs))
    search_rows = jnp.concatenate(search, axis=1)
    gram_rest = jnp.concatenate(
        [
            probe_of(search_rows, given_b) + probe_of(search_rows, given_lo),
            probe_of(search_rows, search_rows),
        ],
        axis=1,
    )
    step = steps_of("fhalf")[0]
    r_sent = jnp.concatenate([sent_half(r_part, "fhalf", step), gram_rest], axis=1)
    r_kept = jnp.concatenate([kept_half(r_part, "fhalf", step), gram_rest], axis=1)
    r_joined = r_kept + swap(r_sent, "fhalf", step)
    joined = after(joined, r_joined)
    half_rows = tok_rows // 2
    d_probe = joined[:, :half_rows]
    x_full = x_probe + joined[:, half_rows : 2 * half_rows]
    gram_given = joined[:, 2 * half_rows :]
    gram_given = jnp.concatenate([gram_given[:, : 2 * cols], gram_given[:, 2 * cols :]], axis=0)
    given_inverse = whiten_given(gram_given / feat_total)
    given_probe = jnp.concatenate([x_full, d_probe], axis=0)
    given_probe_b = jnp.concatenate([x_probe_b, rounded(d_probe)], axis=0)
    raw_given = exact_rows(given_probe, given_probe_b)
    raw_given = jnp.concatenate([raw_given[:cols], raw_given[cols:]], axis=1)
    residual_lo = jnp.concatenate(
        [(residual - high).astype(jnp.bfloat16) for residual, high in zip(residuals, highs)], axis=1
    )
    r_joined = reduce_all(r_joined, "layer")
    r_probe = r_joined[:, :half_rows]
    gram_rest = r_joined[:, half_rows:]
    r_probe_b = rounded(r_probe)
    raw = jnp.concatenate(
        [
            0.5 * (exact_rows(r_probe, given_probe_b) + exact_rows(r_probe_b, given_probe)),
            exact_rows(r_probe, r_probe_b),
            raw_given,
        ],
        axis=1,
    )
    near = steps_of("fhalf")[0]
    side = side_of("fhalf", near)
    raw = lax.dynamic_slice_in_dim(raw, side * (cols // 2), cols // 2, 0) + swap(
        lax.dynamic_slice_in_dim(raw, (1 - side) * (cols // 2), cols // 2, 0), "fhalf", near
    )
    rest_inverse = whiten_rest(given_inverse, after(gram_rest, raw) / feat_total)
    residual_lo = after(residual_lo, raw)
    raw = reduce_all(raw, "token") * ritz_scale
    other = swap(raw, "fhalf", near)
    raw = jnp.concatenate(
        [jnp.where(side == 0, raw, other), jnp.where(side == 0, other, raw)], axis=0
    )
    raw_rest = raw[:, : 3 * cols]
    raw_given = jnp.concatenate([raw[:, 3 * cols : 5 * cols], raw[:, 5 * cols :]], axis=0)
    all_coeffs, ritz_values = ritz_of(given_inverse, rest_inverse, raw_given, raw_rest)
    for step in reversed(token_steps):
        if step == token_steps[0]:
            residual_lo = after(residual_lo, raw)
        residual_lo = joined_halves(residual_lo, "token", step)
    residual_rows = search_rows.astype(jnp.float32) + reordered(residual_lo, CHUNKS).astype(jnp.float32)
    search_basis = jnp.concatenate([x_rows, d_rows, residual_rows], axis=0)
    new_block = moved(all_coeffs[:, :cols], search_basis)
    new_direction = moved(all_coeffs[:, cols:], search_basis)
    return (new_block.T, new_direction.T, ritz_values[0])


def solution(mesh):
    return jax.shard_map(
        local,
        mesh=mesh,
        in_specs=(
            P("token", ("layer", "fhalf")),
            P(("layer", "fhalf"), None),
            P(("layer", "fhalf"), None),
        ),
        out_specs=(P(("layer", "fhalf"), None), P(("layer", "fhalf"), None), P()),
        check_vma=False,
    )
```

```python
import jax
import jax.numpy as jnp
from jax import lax
from jax.experimental import pallas as pl
from jax.experimental.pallas import tpu as pltpu
from jax.sharding import PartitionSpec as P

NSUB = 6
CHUNKS = 2
SPREAD = 1e-4
LARGE = 1e30
HIGHEST = lax.Precision.HIGHEST


def exact_transposed(left, right):
    return lax.dot_general(
        left, right, (((0,), (0,)), ((), ())), precision=HIGHEST, preferred_element_type=jnp.float32
    )


def exact_rows(left, right):
    return lax.dot_general(
        left, right, (((1,), (1,)), ((), ())), precision=HIGHEST, preferred_element_type=jnp.float32
    )


def product(left, right):
    return jnp.dot(left, right, precision=HIGHEST, preferred_element_type=jnp.float32)


def identity(rows, columns):
    down = lax.broadcasted_iota(jnp.int32, (rows, columns), 0)
    across = lax.broadcasted_iota(jnp.int32, (rows, columns), 1)
    return jnp.where(down == across, 1.0, 0.0).astype(jnp.float32)


def factor_inverse(gram):
    size = gram.shape[0]
    wide = jnp.concatenate([gram, identity(size, size)], axis=1)
    tile = (8, 2 * size)
    rows = [wide[8 * g : 8 * g + 8] for g in range(size // 8)]
    sub = lax.broadcasted_iota(jnp.int32, tile, 0)
    done = []
    low = high = total = None
    for g in range(size // 8):
        live = rows[g:]
        panel = [[jnp.broadcast_to(r[:, 8 * g + j : 8 * g + j + 1], tile) for r in live] for j in range(8)]
        scale = None
        for j in range(8):
            head = panel[j][0]
            pivot = jnp.broadcast_to(head[j : j + 1], tile)
            inverse = 1.0 / pivot
            row = jnp.broadcast_to(live[0][j : j + 1], tile)
            factors = [value * inverse for value in panel[j]]
            factors[0] = jnp.where(sub > j, factors[0], 0.0)
            for i in range(j + 1, 8):
                other = jnp.broadcast_to(head[i : i + 1], tile)
                panel[i] = [value - f * other for value, f in zip(panel[i], factors)]
            live = [value - f * row for value, f in zip(live, factors)]
            scale = pivot if scale is None else jnp.where(sub >= j, pivot, scale)
            low = pivot if low is None else jnp.minimum(low, pivot)
            high = pivot if high is None else jnp.maximum(high, pivot)
            total = pivot if total is None else total + pivot
        rows[g:] = live
        done.append(live[0] * lax.rsqrt(scale))
    return jnp.concatenate(done, axis=0)[:, size:], low, high, total


def whiten_given_kernel(gram_ref, out_ref):
    cols = gram_ref.shape[0] // 2
    first = factor_inverse(gram_ref[:cols, :cols])[0]
    lower = exact_rows(gram_ref[cols:, :cols], first)
    second = factor_inverse(gram_ref[cols:, cols:] - exact_rows(lower, lower))[0]
    out_ref[:cols, :cols] = first
    out_ref[:cols, cols:] = jnp.zeros((cols, cols), jnp.float32)
    out_ref[cols:, :cols] = -product(second, product(lower, first))
    out_ref[cols:, cols:] = second


def whiten_given(gram_matrix):
    return pl.pallas_call(
        whiten_given_kernel,
        out_shape=jax.ShapeDtypeStruct(gram_matrix.shape, jnp.float32),
        cost_estimate=pl.CostEstimate(flops=4_000_000_000, transcendentals=0, bytes_accessed=131072),
        name="whiten_given",
    )(gram_matrix)


def whiten_rest_kernel(given_ref, gram_ref, out_ref):
    cols, size = gram_ref.shape
    lower = exact_rows(gram_ref[:, : size - cols], given_ref[...])
    last = factor_inverse(gram_ref[:, size - cols :] - exact_rows(lower, lower))[0]
    out_ref[:, : size - cols] = -product(last, product(lower, given_ref[...]))
    out_ref[:, size - cols :] = last


def whiten_rest(given, gram_rows):
    return pl.pallas_call(
        whiten_rest_kernel,
        out_shape=jax.ShapeDtypeStruct(gram_rows.shape, jnp.float32),
        cost_estimate=pl.CostEstimate(flops=3_000_000_000, transcendentals=0, bytes_accessed=131072),
        name="whiten_rest",
    )(given, gram_rows)


def ritz_kernel(
    given_ref, rest_ref, raw_given_ref, raw_rest_ref, coeffs_ref, values_ref,
    whiten_ref, matrix_ref, power_ref, turned_ref, basis_ref,
):
    size, cols = turned_ref.shape
    rest = size - cols
    whiten_ref[:rest, :rest] = given_ref[...]
    whiten_ref[:rest, rest:] = jnp.zeros((rest, cols), jnp.float32)
    whiten_ref[rest:, :] = rest_ref[...]
    matrix_ref[:rest, :rest] = 0.5 * (raw_given_ref[...] + raw_given_ref[...].T)
    matrix_ref[rest:, :] = raw_rest_ref[...]
    matrix_ref[:rest, rest:] = raw_rest_ref[:, :rest].T
    power_ref[...] = product(whiten_ref[...], matrix_ref[...])
    matrix_ref[...] = exact_rows(power_ref[...], whiten_ref[...])
    matrix_ref[...] = 0.5 * (matrix_ref[...] + matrix_ref[...].T)
    power_ref[...] = product(matrix_ref[...], matrix_ref[...])
    power_ref[...] = product(power_ref[...], matrix_ref[...])

    def sweep(step_ref, count):
        def turn(number, good):
            @pl.when(number == 0)
            def _():
                turned_ref[...] = step_ref[:, :cols]

            @pl.when(number > 0)
            def _():
                turned_ref[...] = product(step_ref[...], basis_ref[...])

            turned = turned_ref[...]
            inverse, low, high, total = factor_inverse(exact_transposed(turned, turned))
            basis_ref[...] = exact_rows(turned_ref[...], inverse)
            fine = jnp.logical_and(low > SPREAD * high, total < LARGE)
            return jnp.minimum(good, jnp.where(fine, 1.0, 0.0))

        return lax.fori_loop(0, count, turn, jnp.ones((8, 2 * cols), jnp.float32))

    good = jnp.min(sweep(power_ref, NSUB // 3))

    @pl.when(good < 0.5)
    def _():
        sweep(matrix_ref, NSUB)

    values_ref[...] = jnp.sum(
        basis_ref[...] * product(matrix_ref[...], basis_ref[...]), axis=0, keepdims=True
    )
    down = lax.broadcasted_iota(jnp.int32, (size, cols), 0)
    power_ref[:, :cols] = basis_ref[...]
    power_ref[:, cols : 2 * cols] = jnp.where(down >= cols, basis_ref[...], 0.0)
    coeffs_ref[...] = exact_transposed(whiten_ref[...], power_ref[:, : 2 * cols])


def ritz_of(given, rest, raw_given, raw_rest):
    cols, size = rest.shape
    return pl.pallas_call(
        ritz_kernel,
        out_shape=(
            jax.ShapeDtypeStruct((size, 2 * cols), jnp.float32),
            jax.ShapeDtypeStruct((1, cols), jnp.float32),
        ),
        scratch_shapes=[
            pltpu.VMEM((size, size), jnp.float32),
            pltpu.VMEM((size, size), jnp.float32),
            pltpu.VMEM((size, size), jnp.float32),
            pltpu.VMEM((size, cols), jnp.float32),
            pltpu.VMEM((size, cols), jnp.float32),
        ],
        cost_estimate=pl.CostEstimate(flops=10_000_000_000, transcendentals=0, bytes_accessed=524288),
        name="ritz",
    )(given, rest, raw_given, raw_rest)


def rounded(value):
    return lax.reduce_precision(value, exponent_bits=8, mantissa_bits=7)


def moved(coeffs, rows):
    return lax.dot_general(
        coeffs,
        rows,
        (((0,), (0,)), ((), ())),
        precision=lax.Precision.HIGH,
        preferred_element_type=jnp.float32,
    )


def swap(value, axis, step):
    return lax.ppermute(value, axis, [(i, i ^ step) for i in range(lax.axis_size(axis))])


def steps_of(axis):
    size = lax.axis_size(axis)
    if size & (size - 1):
        raise ValueError(axis)
    return [1 << bit for bit in range(size.bit_length() - 1)]


def reduce_all(value, axis):
    size = lax.axis_size(axis)
    if size == 4:
        near, far, across = (swap(value, axis, step) for step in (1, 2, 3))
        return (value + near) + (far + across)
    for step in steps_of(axis):
        value = value + swap(value, axis, step)
    return value


def side_of(axis, step):
    return (lax.axis_index(axis) // step) % 2


def sent_half(value, axis, step):
    half = value.shape[1] // 2
    return lax.dynamic_slice_in_dim(value, (1 - side_of(axis, step)) * half, half, 1)


def kept_half(value, axis, step):
    half = value.shape[1] // 2
    return lax.dynamic_slice_in_dim(value, side_of(axis, step) * half, half, 1)


def reduce_halves(value, axis):
    for step in steps_of(axis):
        value = kept_half(value, axis, step) + swap(sent_half(value, axis, step), axis, step)
    return value


def own_part(value, axis):
    for step in steps_of(axis):
        value = kept_half(value, axis, step)
    return value


def joined_halves(value, axis, step):
    other = swap(value, axis, step)
    first = side_of(axis, step) == 0
    return jnp.concatenate([jnp.where(first, value, other), jnp.where(first, other, value)], axis=1)


def gather_halves(value, axis):
    for step in reversed(steps_of(axis)):
        value = joined_halves(value, axis, step)
    return value


def probe_of(rows_b, slab_part):
    return lax.dot_general(
        rows_b, slab_part, (((1,), (1,)), ((), ())), preferred_element_type=jnp.float32
    )


def reordered(value, chunks):
    rows, width = value.shape
    devices = lax.axis_size("token")
    piece = width // (chunks * devices)
    pieces = [
        [value[:, piece * (chunks * d + c) : piece * (chunks * d + c) + piece] for d in range(devices)]
        for c in range(chunks)
    ]
    return jnp.concatenate([p for line in pieces for p in line], axis=1)


def after(value, *earlier):
    return lax.optimization_barrier((value, *earlier))[0]


def local(hidden_slab, current_block, direction):
    tok_rows, half_width = hidden_slab.shape
    cols = current_block.shape[1]
    feat_total = half_width * lax.axis_size("layer") * lax.axis_size("fhalf")
    token_total = tok_rows * lax.axis_size("token")
    ritz_scale = 1.0 / (token_total * feat_total)
    x_rows = current_block.T
    d_rows = direction.T
    chunk = half_width // CHUNKS
    starts = [chunk * c for c in range(CHUNKS)]
    slabs = [hidden_slab[:, at : at + chunk] for at in starts]
    given_rows = jnp.concatenate([x_rows, d_rows], axis=0)
    given_hi = rounded(given_rows)
    given_b = given_hi.astype(jnp.bfloat16)
    given_lo = (given_rows - given_hi).astype(jnp.bfloat16)
    given_part = probe_of(jnp.concatenate([given_b, given_lo[:cols]], axis=0), hidden_slab)
    x_probe = reduce_all(reduce_halves(given_part[:cols], "fhalf"), "layer")
    x_probe_b = rounded(x_probe)
    block_probe = gather_halves(x_probe_b.astype(jnp.bfloat16), "fhalf")
    token_steps = steps_of("token")
    parts, sents = [], []
    for slab in slabs:
        probe = after(block_probe, sents[-1]) if sents else block_probe
        part = jnp.dot(probe, slab, preferred_element_type=jnp.float32)
        sent = sent_half(part, "token", token_steps[0])
        if not parts:
            ritz_block = probe_of(block_probe, block_probe)
            sent = jnp.concatenate([sent, ritz_block], axis=1)
        parts.append(part)
        sents.append(sent)
    for number, step in enumerate(token_steps):
        images = []
        for c in range(CHUNKS):
            got = swap(sents[c], "token", step)
            if c == 0:
                ritz_block = ritz_block + got[:, got.shape[1] - cols :]
                got = got[:, : got.shape[1] - cols]
            images.append(kept_half(parts[c], "token", step) + got)
        parts = images
        if number + 1 < len(token_steps):
            sents = [sent_half(part, "token", token_steps[number + 1]) for part in parts]
            sents[0] = jnp.concatenate([sents[0], ritz_block], axis=1)
        if number == 0:
            d_part, late_rows = lax.optimization_barrier((given_part[cols:], given_rows, sents[0]))[:2]
            gram_given = exact_rows(late_rows, late_rows)
            gram_given = jnp.concatenate([gram_given[:cols], gram_given[cols:]], axis=1)
            near = steps_of("fhalf")[0]
            joined_sent, joined_kept = (
                jnp.concatenate([half[:cols], half[cols:], gram_given], axis=1)
                for half in (sent_half(d_part, "fhalf", near), kept_half(d_part, "fhalf", near))
            )
            joined = joined_kept + swap(joined_sent, "fhalf", near)
            joined = after(joined, *sents)
    ritz_block = ritz_block * ritz_scale
    residuals = [
        image / token_total
        - exact_transposed(ritz_block, own_part(x_rows[:, at : at + chunk], "token"))
        for image, at in zip(images, starts)
    ]
    highs = [rounded(residual) for residual in residuals]
    high_b = [high.astype(jnp.bfloat16) for high in highs]
    joined = reduce_all(joined, "layer")
    search = []
    for number, rows in enumerate(high_b):
        for step in reversed(token_steps):
            if step == token_steps[-1] and number + 1 == CHUNKS:
                rows = after(rows, joined)
            rows = joined_halves(rows, "token", step)
        search.append(rows)
    r_part = sum(probe_of(rows, slab) for rows, slab in zip(search, slabs))
    search_rows = jnp.concatenate(search, axis=1)
    gram_rest = jnp.concatenate(
        [
            probe_of(search_rows, given_b) + probe_of(search_rows, given_lo),
            probe_of(search_rows, search_rows),
        ],
        axis=1,
    )
    step = steps_of("fhalf")[0]
    r_sent = jnp.concatenate([sent_half(r_part, "fhalf", step), gram_rest], axis=1)
    r_kept = jnp.concatenate([kept_half(r_part, "fhalf", step), gram_rest], axis=1)
    r_joined = r_kept + swap(r_sent, "fhalf", step)
    joined = after(joined, r_joined)
    half_rows = tok_rows // 2
    d_probe = joined[:, :half_rows]
    x_full = x_probe + joined[:, half_rows : 2 * half_rows]
    gram_given = joined[:, 2 * half_rows :]
    gram_given = jnp.concatenate([gram_given[:, : 2 * cols], gram_given[:, 2 * cols :]], axis=0)
    given_inverse = whiten_given(gram_given / feat_total)
    given_probe = jnp.concatenate([x_full, d_probe], axis=0)
    given_probe_b = jnp.concatenate([x_probe_b, rounded(d_probe)], axis=0)
    raw_given = exact_rows(given_probe, given_probe_b)
    raw_given = jnp.concatenate([raw_given[:cols], raw_given[cols:]], axis=1)
    residual_lo = jnp.concatenate(
        [(residual - high).astype(jnp.bfloat16) for residual, high in zip(residuals, highs)], axis=1
    )
    r_joined = after(reduce_all(r_joined, "layer"), given_inverse)
    r_probe = r_joined[:, :half_rows]
    gram_rest = r_joined[:, half_rows:]
    r_probe_b = rounded(r_probe)
    raw = jnp.concatenate(
        [
            0.5 * (exact_rows(r_probe, given_probe_b) + exact_rows(r_probe_b, given_probe)),
            exact_rows(r_probe, r_probe_b),
            raw_given,
        ],
        axis=1,
    )
    near = steps_of("fhalf")[0]
    side = side_of("fhalf", near)
    raw = lax.dynamic_slice_in_dim(raw, side * (cols // 2), cols // 2, 0) + swap(
        lax.dynamic_slice_in_dim(raw, (1 - side) * (cols // 2), cols // 2, 0), "fhalf", near
    )
    rest_inverse = whiten_rest(given_inverse, after(gram_rest, raw) / feat_total)
    residual_lo = after(residual_lo, raw)
    for step in reversed(token_steps[1:]):
        residual_lo = joined_halves(residual_lo, "token", step)
    raw = after(reduce_all(raw, "token") * ritz_scale, rest_inverse, residual_lo)
    other = swap(raw, "fhalf", near)
    raw = jnp.concatenate(
        [jnp.where(side == 0, raw, other), jnp.where(side == 0, other, raw)], axis=0
    )
    raw_rest = raw[:, : 3 * cols]
    raw_given = jnp.concatenate([raw[:, 3 * cols : 5 * cols], raw[:, 5 * cols :]], axis=0)
    all_coeffs, ritz_values = ritz_of(given_inverse, rest_inverse, raw_given, raw_rest)
    residual_lo = joined_halves(after(residual_lo, raw), "token", token_steps[0])
    residual_rows = search_rows.astype(jnp.float32) + reordered(residual_lo, CHUNKS).astype(jnp.float32)
    search_basis = jnp.concatenate([x_rows, d_rows, residual_rows], axis=0)
    new_block = moved(all_coeffs[:, :cols], search_basis)
    new_direction = moved(all_coeffs[:, cols:], search_basis)
    return (new_block.T, new_direction.T, ritz_values[0])


def solution(mesh):
    return jax.shard_map(
        local,
        mesh=mesh,
        in_specs=(
            P("token", ("layer", "fhalf")),
            P(("layer", "fhalf"), None),
            P(("layer", "fhalf"), None),
        ),
        out_specs=(P(("layer", "fhalf"), None), P(("layer", "fhalf"), None), P()),
        check_vma=False,
    )
```

```python
import jax
import jax.numpy as jnp
from jax import lax
from jax.experimental import pallas as pl
from jax.experimental.pallas import tpu as pltpu
from jax.sharding import PartitionSpec as P

NSUB = 6
CHUNKS = 2
SPREAD = 1e-4
LARGE = 1e30
HIGHEST = lax.Precision.HIGHEST


def exact_transposed(left, right):
    return lax.dot_general(
        left, right, (((0,), (0,)), ((), ())), precision=HIGHEST, preferred_element_type=jnp.float32
    )


def exact_rows(left, right):
    return lax.dot_general(
        left, right, (((1,), (1,)), ((), ())), precision=HIGHEST, preferred_element_type=jnp.float32
    )


def product(left, right):
    return jnp.dot(left, right, precision=HIGHEST, preferred_element_type=jnp.float32)


def identity(rows, columns):
    down = lax.broadcasted_iota(jnp.int32, (rows, columns), 0)
    across = lax.broadcasted_iota(jnp.int32, (rows, columns), 1)
    return jnp.where(down == across, 1.0, 0.0).astype(jnp.float32)


def factor_inverse(gram):
    size = gram.shape[0]
    wide = jnp.concatenate([gram, identity(size, size)], axis=1)
    tile = (8, 2 * size)
    rows = [wide[8 * g : 8 * g + 8] for g in range(size // 8)]
    sub = lax.broadcasted_iota(jnp.int32, tile, 0)
    done = []
    low = high = total = None
    for g in range(size // 8):
        live = rows[g:]
        panel = [[jnp.broadcast_to(r[:, 8 * g + j : 8 * g + j + 1], tile) for r in live] for j in range(8)]
        scale = None
        for j in range(8):
            head = panel[j][0]
            pivot = jnp.broadcast_to(head[j : j + 1], tile)
            inverse = 1.0 / pivot
            row = jnp.broadcast_to(live[0][j : j + 1], tile)
            factors = [value * inverse for value in panel[j]]
            factors[0] = jnp.where(sub > j, factors[0], 0.0)
            for i in range(j + 1, 8):
                other = jnp.broadcast_to(head[i : i + 1], tile)
                panel[i] = [value - f * other for value, f in zip(panel[i], factors)]
            live = [value - f * row for value, f in zip(live, factors)]
            scale = pivot if scale is None else jnp.where(sub >= j, pivot, scale)
            low = pivot if low is None else jnp.minimum(low, pivot)
            high = pivot if high is None else jnp.maximum(high, pivot)
            total = pivot if total is None else total + pivot
        rows[g:] = live
        done.append(live[0] * lax.rsqrt(scale))
    return jnp.concatenate(done, axis=0)[:, size:], low, high, total


def whiten_given_kernel(gram_ref, out_ref):
    cols = gram_ref.shape[0] // 2
    first = factor_inverse(gram_ref[:cols, :cols])[0]
    lower = exact_rows(gram_ref[cols:, :cols], first)
    second = factor_inverse(gram_ref[cols:, cols:] - exact_rows(lower, lower))[0]
    out_ref[:cols, :cols] = first
    out_ref[:cols, cols:] = jnp.zeros((cols, cols), jnp.float32)
    out_ref[cols:, :cols] = -product(second, product(lower, first))
    out_ref[cols:, cols:] = second


def whiten_given(gram_matrix):
    return pl.pallas_call(
        whiten_given_kernel,
        out_shape=jax.ShapeDtypeStruct(gram_matrix.shape, jnp.float32),
        cost_estimate=pl.CostEstimate(flops=4_000_000_000, transcendentals=0, bytes_accessed=131072),
        name="whiten_given",
    )(gram_matrix)


def whiten_rest_kernel(given_ref, gram_ref, out_ref):
    cols, size = gram_ref.shape
    lower = exact_rows(gram_ref[:, : size - cols], given_ref[...])
    last = factor_inverse(gram_ref[:, size - cols :] - exact_rows(lower, lower))[0]
    out_ref[:, : size - cols] = -product(last, product(lower, given_ref[...]))
    out_ref[:, size - cols :] = last


def whiten_rest(given, gram_rows):
    return pl.pallas_call(
        whiten_rest_kernel,
        out_shape=jax.ShapeDtypeStruct(gram_rows.shape, jnp.float32),
        cost_estimate=pl.CostEstimate(flops=3_000_000_000, transcendentals=0, bytes_accessed=131072),
        name="whiten_rest",
    )(given, gram_rows)


def ritz_kernel(
    given_ref, rest_ref, raw_given_ref, raw_rest_ref, coeffs_ref, values_ref,
    whiten_ref, matrix_ref, power_ref, turned_ref, basis_ref,
):
    size, cols = turned_ref.shape
    rest = size - cols
    whiten_ref[:rest, :rest] = given_ref[...]
    whiten_ref[:rest, rest:] = jnp.zeros((rest, cols), jnp.float32)
    whiten_ref[rest:, :] = rest_ref[...]
    matrix_ref[:rest, :rest] = 0.5 * (raw_given_ref[...] + raw_given_ref[...].T)
    matrix_ref[rest:, :] = raw_rest_ref[...]
    matrix_ref[:rest, rest:] = raw_rest_ref[:, :rest].T
    power_ref[...] = product(whiten_ref[...], matrix_ref[...])
    matrix_ref[...] = exact_rows(power_ref[...], whiten_ref[...])
    matrix_ref[...] = 0.5 * (matrix_ref[...] + matrix_ref[...].T)
    power_ref[...] = product(matrix_ref[...], matrix_ref[...])
    power_ref[...] = product(power_ref[...], matrix_ref[...])

    def sweep(step_ref, count):
        def turn(number, good):
            @pl.when(number == 0)
            def _():
                turned_ref[...] = step_ref[:, :cols]

            @pl.when(number > 0)
            def _():
                turned_ref[...] = product(step_ref[...], basis_ref[...])

            turned = turned_ref[...]
            inverse, low, high, total = factor_inverse(exact_transposed(turned, turned))
            basis_ref[...] = exact_rows(turned_ref[...], inverse)
            fine = jnp.logical_and(low > SPREAD * high, total < LARGE)
            return jnp.minimum(good, jnp.where(fine, 1.0, 0.0))

        return lax.fori_loop(0, count, turn, jnp.ones((8, 2 * cols), jnp.float32))

    good = jnp.min(sweep(power_ref, NSUB // 3))

    @pl.when(good < 0.5)
    def _():
        sweep(matrix_ref, NSUB)

    values_ref[...] = jnp.sum(
        basis_ref[...] * product(matrix_ref[...], basis_ref[...]), axis=0, keepdims=True
    )
    down = lax.broadcasted_iota(jnp.int32, (size, cols), 0)
    power_ref[:, :cols] = basis_ref[...]
    power_ref[:, cols : 2 * cols] = jnp.where(down >= cols, basis_ref[...], 0.0)
    coeffs_ref[...] = exact_transposed(whiten_ref[...], power_ref[:, : 2 * cols])


def ritz_of(given, rest, raw_given, raw_rest):
    cols, size = rest.shape
    return pl.pallas_call(
        ritz_kernel,
        out_shape=(
            jax.ShapeDtypeStruct((size, 2 * cols), jnp.float32),
            jax.ShapeDtypeStruct((1, cols), jnp.float32),
        ),
        scratch_shapes=[
            pltpu.VMEM((size, size), jnp.float32),
            pltpu.VMEM((size, size), jnp.float32),
            pltpu.VMEM((size, size), jnp.float32),
            pltpu.VMEM((size, cols), jnp.float32),
            pltpu.VMEM((size, cols), jnp.float32),
        ],
        cost_estimate=pl.CostEstimate(flops=10_000_000_000, transcendentals=0, bytes_accessed=524288),
        name="ritz",
    )(given, rest, raw_given, raw_rest)


def rounded(value):
    return lax.reduce_precision(value, exponent_bits=8, mantissa_bits=7)


def moved(coeffs, rows):
    return lax.dot_general(
        coeffs,
        rows,
        (((0,), (0,)), ((), ())),
        precision=lax.Precision.HIGH,
        preferred_element_type=jnp.float32,
    )


def swap(value, axis, step):
    return lax.ppermute(value, axis, [(i, i ^ step) for i in range(lax.axis_size(axis))])


def steps_of(axis):
    size = lax.axis_size(axis)
    if size & (size - 1):
        raise ValueError(axis)
    return [1 << bit for bit in range(size.bit_length() - 1)]


def reduce_all(value, axis):
    size = lax.axis_size(axis)
    if size == 4:
        near, far, across = (swap(value, axis, step) for step in (1, 2, 3))
        return (value + near) + (far + across)
    for step in steps_of(axis):
        value = value + swap(value, axis, step)
    return value


def side_of(axis, step):
    return (lax.axis_index(axis) // step) % 2


def sent_half(value, axis, step):
    half = value.shape[1] // 2
    return lax.dynamic_slice_in_dim(value, (1 - side_of(axis, step)) * half, half, 1)


def kept_half(value, axis, step):
    half = value.shape[1] // 2
    return lax.dynamic_slice_in_dim(value, side_of(axis, step) * half, half, 1)


def reduce_halves(value, axis):
    for step in steps_of(axis):
        value = kept_half(value, axis, step) + swap(sent_half(value, axis, step), axis, step)
    return value


def own_part(value, axis):
    for step in steps_of(axis):
        value = kept_half(value, axis, step)
    return value


def gather_direct(value, axis):
    if lax.axis_size(axis) != 4:
        return gather_halves(value, axis)
    near, far, across = (swap(value, axis, step) for step in (1, 2, 3))
    return beside(beside(value, far, axis, 2), beside(near, across, axis, 2), axis, 1)


def joined_halves(value, axis, step):
    return beside(value, swap(value, axis, step), axis, step)


def beside(value, other, axis, step):
    first = side_of(axis, step) == 0
    return jnp.concatenate([jnp.where(first, value, other), jnp.where(first, other, value)], axis=1)


def gather_halves(value, axis):
    for step in reversed(steps_of(axis)):
        value = joined_halves(value, axis, step)
    return value


def probe_of(rows_b, slab_part):
    return lax.dot_general(
        rows_b, slab_part, (((1,), (1,)), ((), ())), preferred_element_type=jnp.float32
    )


def reordered(value, chunks):
    rows, width = value.shape
    devices = lax.axis_size("token")
    piece = width // (chunks * devices)
    pieces = [
        [value[:, piece * (chunks * d + c) : piece * (chunks * d + c) + piece] for d in range(devices)]
        for c in range(chunks)
    ]
    return jnp.concatenate([p for line in pieces for p in line], axis=1)


def after(value, *earlier):
    return lax.optimization_barrier((value, *earlier))[0]


def local(hidden_slab, current_block, direction):
    tok_rows, half_width = hidden_slab.shape
    cols = current_block.shape[1]
    feat_total = half_width * lax.axis_size("layer") * lax.axis_size("fhalf")
    token_total = tok_rows * lax.axis_size("token")
    ritz_scale = 1.0 / (token_total * feat_total)
    x_rows = current_block.T
    d_rows = direction.T
    chunk = half_width // CHUNKS
    starts = [chunk * c for c in range(CHUNKS)]
    slabs = [hidden_slab[:, at : at + chunk] for at in starts]
    given_rows = jnp.concatenate([x_rows, d_rows], axis=0)
    given_hi = rounded(given_rows)
    given_b = given_hi.astype(jnp.bfloat16)
    given_lo = (given_rows - given_hi).astype(jnp.bfloat16)
    given_part = probe_of(jnp.concatenate([given_b, given_lo[:cols]], axis=0), hidden_slab)
    x_probe = reduce_all(reduce_halves(given_part[:cols], "fhalf"), "layer")
    x_probe_b = rounded(x_probe)
    block_probe = gather_halves(x_probe_b.astype(jnp.bfloat16), "fhalf")
    token_steps = steps_of("token")
    parts, sents = [], []
    for slab in slabs:
        probe = after(block_probe, sents[-1]) if sents else block_probe
        part = jnp.dot(probe, slab, preferred_element_type=jnp.float32)
        sent = sent_half(part, "token", token_steps[0])
        if not parts:
            ritz_block = probe_of(block_probe, block_probe)
            sent = jnp.concatenate([sent, ritz_block], axis=1)
        parts.append(part)
        sents.append(sent)
    for number, step in enumerate(token_steps):
        images = []
        for c in range(CHUNKS):
            got = swap(sents[c], "token", step)
            if c == 0:
                ritz_block = ritz_block + got[:, got.shape[1] - cols :]
                got = got[:, : got.shape[1] - cols]
            images.append(kept_half(parts[c], "token", step) + got)
        parts = images
        if number + 1 < len(token_steps):
            sents = [sent_half(part, "token", token_steps[number + 1]) for part in parts]
            sents[0] = jnp.concatenate([sents[0], ritz_block], axis=1)
        if number == 0:
            d_part, late_rows = lax.optimization_barrier((given_part[cols:], given_rows, sents[0]))[:2]
            gram_given = exact_rows(late_rows, late_rows)
            gram_given = jnp.concatenate([gram_given[:cols], gram_given[cols:]], axis=1)
            near = steps_of("fhalf")[0]
            joined_sent, joined_kept = (
                jnp.concatenate([half[:cols], half[cols:], gram_given], axis=1)
                for half in (sent_half(d_part, "fhalf", near), kept_half(d_part, "fhalf", near))
            )
            joined = joined_kept + swap(joined_sent, "fhalf", near)
            joined = after(joined, *sents)
    ritz_block = ritz_block * ritz_scale
    residuals = [
        image / token_total
        - exact_transposed(ritz_block, own_part(x_rows[:, at : at + chunk], "token"))
        for image, at in zip(images, starts)
    ]
    highs = [rounded(residual) for residual in residuals]
    high_b = [high.astype(jnp.bfloat16) for high in highs]
    search = [gather_halves(high, "token") for high in high_b]
    joined = reduce_all(joined, "layer")
    r_part = sum(probe_of(rows, slab) for rows, slab in zip(search, slabs))
    search_rows = jnp.concatenate(search, axis=1)
    gram_rest = jnp.concatenate(
        [
            probe_of(search_rows, given_b) + probe_of(search_rows, given_lo),
            probe_of(search_rows, search_rows),
        ],
        axis=1,
    )
    step = steps_of("fhalf")[0]
    r_sent = jnp.concatenate([sent_half(r_part, "fhalf", step), gram_rest], axis=1)
    r_kept = jnp.concatenate([kept_half(r_part, "fhalf", step), gram_rest], axis=1)
    r_joined = r_kept + swap(r_sent, "fhalf", step)
    joined = after(joined, r_joined)
    half_rows = tok_rows // 2
    d_probe = joined[:, :half_rows]
    x_full = x_probe + joined[:, half_rows : 2 * half_rows]
    gram_given = joined[:, 2 * half_rows :]
    gram_given = jnp.concatenate([gram_given[:, : 2 * cols], gram_given[:, 2 * cols :]], axis=0)
    given_inverse = whiten_given(gram_given / feat_total)
    given_probe = jnp.concatenate([x_full, d_probe], axis=0)
    given_probe_b = jnp.concatenate([x_probe_b, rounded(d_probe)], axis=0)
    raw_given = exact_rows(given_probe, given_probe_b)
    raw_given = jnp.concatenate([raw_given[:cols], raw_given[cols:]], axis=1)
    residual_lo = jnp.concatenate(
        [(residual - high).astype(jnp.bfloat16) for residual, high in zip(residuals, highs)], axis=1
    )
    residual_lo = after(residual_lo, r_part)
    r_joined = reduce_all(r_joined, "layer")
    r_probe = r_joined[:, :half_rows]
    gram_rest = r_joined[:, half_rows:]
    r_probe_b = rounded(r_probe)
    raw = jnp.concatenate(
        [
            0.5 * (exact_rows(r_probe, given_probe_b) + exact_rows(r_probe_b, given_probe)),
            exact_rows(r_probe, r_probe_b),
            raw_given,
        ],
        axis=1,
    )
    near = steps_of("fhalf")[0]
    side = side_of("fhalf", near)
    raw = lax.dynamic_slice_in_dim(raw, side * (cols // 2), cols // 2, 0) + swap(
        lax.dynamic_slice_in_dim(raw, (1 - side) * (cols // 2), cols // 2, 0), "fhalf", near
    )
    rest_inverse = whiten_rest(given_inverse, after(gram_rest, raw) / feat_total)
    raw = reduce_all(raw, "token") * ritz_scale
    other = swap(raw, "fhalf", near)
    raw = jnp.concatenate(
        [jnp.where(side == 0, raw, other), jnp.where(side == 0, other, raw)], axis=0
    )
    raw_rest = raw[:, : 3 * cols]
    raw_given = jnp.concatenate([raw[:, 3 * cols : 5 * cols], raw[:, 5 * cols :]], axis=0)
    all_coeffs, ritz_values = ritz_of(given_inverse, rest_inverse, raw_given, raw_rest)
    residual_lo = gather_direct(residual_lo, "token")
    residual_rows = search_rows.astype(jnp.float32) + reordered(residual_lo, CHUNKS).astype(jnp.float32)
    search_basis = jnp.concatenate([x_rows, d_rows, residual_rows], axis=0)
    new_block = moved(all_coeffs[:, :cols], search_basis)
    new_direction = moved(all_coeffs[:, cols:], search_basis)
    return (new_block.T, new_direction.T, ritz_values[0])


def solution(mesh):
    return jax.shard_map(
        local,
        mesh=mesh,
        in_specs=(
            P("token", ("layer", "fhalf")),
            P(("layer", "fhalf"), None),
            P(("layer", "fhalf"), None),
        ),
        out_specs=(P(("layer", "fhalf"), None), P(("layer", "fhalf"), None), P()),
        check_vma=False,
    )
```
